128 devices in a mesh: req: 4 (over z), vocab: 32 (over y, x, core).
Axes of the slice: x: 4, y: 4, z: 4, core: 2. Of those that a mesh axis runs over, the one named last changes fastest.
Arguments:
- hidden_states: bfloat16 [24576, 2048], P(('req', 'vocab')), may hold values from -400 to 400
- norm_gain: float32 [2048], replicated, may hold values from 0.25 to 1.75
- head_weight: bfloat16 [2048, 32000], P(None, 'vocab'), may hold values from -2 to 2
- targets: int32 [24576], P(('req', 'vocab')), may hold values from 0 to 31999
- lengths: int32 [1024], P(('req', 'vocab')), may hold values from 1 to 24, as said below
- slot_of: int32 [1024], P(('req', 'vocab')), may hold values from 0 to 1023, each once
Outputs:
- logprob: float32 [1024, 24], P(('req', 'vocab'))
- entropy: float32 [1024, 24], P(('req', 'vocab'))
The draws below stay inside these ranges and needn't reach their ends.
Inputs may be any that keep to these rules, and one draw needn't show every extreme that they name: The lengths of the 8 requests of one device sum to at most 128; some device's sum to exactly 128.
All inputs are finite; a program needn't handle non-finite values.
Results may differ from the reference program's by a relative error of at most 0.00097.
Values may be sent and summed in bfloat16 or wider, within the bound.
A program may use at most 128 MiB of HBM per device.

```python
import math
import jax
import jax.numpy as jnp
import numpy as np
from jax import lax

D = 2048
V = 32000
SEQ_DEV = 8
SEQ_LEN = 24
LIVE_CAP = 128
SEQS = 1024
ROWS = 24576


def draw_hidden_states(key, part):
    subkeys = jax.random.split(jax.random.fold_in(key, 11), 3)
    rows_total = SEQS * SEQ_LEN
    random_part = jnp.clip(jax.random.normal(subkeys[0], (rows_total, D), jnp.float32), -4.0, 4.0)
    log_top = jnp.log(10.0)
    row_scale = jnp.exp(jax.random.uniform(subkeys[1], (rows_total, 1), jnp.float32, 0.0, 1.0) * log_top)
    col_scale = jnp.exp(jax.random.uniform(subkeys[2], (1, D), jnp.float32, 0.0, 1.0) * jnp.log(10.0))
    values = random_part * row_scale * col_scale
    return values.astype(jnp.bfloat16)


def draw_head_weight(key, part):
    weight_key = jax.random.fold_in(key, 23)
    weight = jnp.clip(jax.random.normal(weight_key, (D, V), jnp.float32), -4.0, 4.0) * (3.0 / jnp.sqrt(float(D)))
    return weight.astype(jnp.bfloat16)


def draw_lengths(key, part):
    subkeys = jax.random.split(jax.random.fold_in(key, 37), SEQ_DEV + 2)
    owners = SEQS // SEQ_DEV
    budget = jax.random.randint(subkeys[0], (owners,), SEQ_DEV, LIVE_CAP + 1)
    fullest = jax.random.randint(subkeys[1], (), 0, owners)
    owner_ids = jnp.arange(owners, dtype=jnp.int32)
    budget = jnp.where(owner_ids == fullest, LIVE_CAP, budget)
    budget = jnp.where(owner_ids == (fullest + 1) % owners, SEQ_DEV, budget)
    remaining = budget
    pieces = []
    for request in range(SEQ_DEV):
        after = SEQ_DEV - 1 - request
        lowest = jnp.maximum(1, remaining - after * SEQ_LEN)
        highest = jnp.minimum(SEQ_LEN, remaining - after)
        chosen = jax.random.randint(subkeys[request + 2], (owners,), lowest, highest + 1)
        if request == 0:
            chosen = jnp.where(owner_ids == fullest, min(SEQ_LEN, LIVE_CAP), chosen)
        pieces.append(chosen)
        remaining = remaining - chosen
    return jnp.stack(pieces, axis=1).reshape(SEQS).astype(jnp.int32)


def touch_ends(entries, key, least, top_value):
    shape = entries.shape
    index_at = [jax.random.randint(jax.random.fold_in(key, axis), (), 0, shape[axis]) for axis in range(len(shape))]
    entries = entries.at[tuple(index_at)].set(least)
    longest = shape.index(max(shape))
    index_at[longest] = (index_at[longest] + 1) % shape[longest]
    return entries.at[tuple(index_at)].set(top_value)


def rank_table(number_of, slope):
    weights = [(1 << 20) // math.isqrt(grade ** slope) + 1 for grade in range(1, number_of + 1)]
    scale = 1 + sum(weights) // (1 << 30)
    return np.cumsum(np.array([max(1, weight // scale) for weight in weights]))


def ranked_ids(stream_key, shape, count, slope):
    table = rank_table(count, slope)
    lot = jax.random.randint(jax.random.fold_in(stream_key, 1), shape, 0, int(table[count - 1]))
    grade = jnp.searchsorted(jnp.asarray(table, jnp.int32), lot, side="right")
    return jax.random.permutation(jax.random.fold_in(stream_key, 2), count)[grade].astype(jnp.int32)


def setup_inputs(seed: int = 0) -> dict:
    seeds = jax.random.split(jax.random.key(seed), 7)
    return {
        "hidden_states": draw_hidden_states(jax.random.fold_in(seeds[6], 71), 0),
        "norm_gain": jnp.clip(1.0 + 0.15 * jax.random.normal(seeds[1], (D,), jnp.float32), 0.25, 1.75),
        "head_weight": draw_head_weight(jax.random.fold_in(seeds[6], 71), 0),
        "targets": touch_ends(ranked_ids(seeds[3], (ROWS,), V, 2), jax.random.fold_in(seeds[3], 3), 0, V - 1).astype(jnp.int32),
        "lengths": draw_lengths(jax.random.fold_in(seeds[6], 71), 0),
        "slot_of": jax.random.permutation(seeds[5], SEQS).astype(jnp.int32),
    }


eps_norm = 1e-05

def reference(hidden_states, norm_gain, head_weight, targets, lengths, slot_of):
    values = hidden_states.astype(jnp.float32)
    inverse_rms = lax.rsqrt(lax.optimization_barrier(jnp.mean(values * values, axis=1, keepdims=True)) + eps_norm)
    normed = (values * inverse_rms * norm_gain[None, :]).astype(jnp.bfloat16)
    block_count = SEQS // SEQ_DEV
    block_size = SEQ_DEV * SEQ_LEN

    def one_block(block_pair):
        block_rows, block_targets = block_pair
        logits = jnp.dot(block_rows, head_weight, preferred_element_type=jnp.float32)
        row_peak = lax.optimization_barrier(jnp.max(logits, axis=1))
        shifted = logits - row_peak[:, None]
        exponent = jnp.exp(shifted)
        row_total = lax.optimization_barrier(jnp.sum(exponent, axis=1))
        spread = lax.optimization_barrier(jnp.sum(exponent * shifted, axis=1))
        picked = jnp.take_along_axis(logits, block_targets[:, None].astype(jnp.int32), axis=1)[:, 0]
        log_total = jnp.log(row_total)
        return (picked - row_peak - log_total, log_total - spread / row_total)
    slot_logprob, slot_entropy = lax.map(one_block, (normed.reshape(block_count, block_size, D), targets.reshape(block_count, block_size)))
    slot_logprob = slot_logprob.reshape(SEQS, SEQ_LEN)
    slot_entropy = slot_entropy.reshape(SEQS, SEQ_LEN)
    live_mask = jnp.arange(SEQ_LEN, dtype=jnp.int32)[None, :] < lengths[:, None]
    slot_logprob = jnp.where(live_mask, slot_logprob, jnp.zeros_like(slot_logprob))
    slot_entropy = jnp.where(live_mask, slot_entropy, jnp.zeros_like(slot_entropy))
    return (slot_logprob[slot_of], slot_entropy[slot_of])
```

```python
import jax
import jax.numpy as jnp
from jax import lax
from jax.experimental import pallas as pl
from jax.experimental.pallas import tpu as pltpu

eps_norm = 1e-05
side = 4
cap = 128
pieces = 2
piece_rows = cap // pieces
mesh_ids = pl.DeviceIdType.MESH
f32 = jnp.float32

group_order = [(0, 0), (0, 1), (1, 0), (0, 3), (3, 0), (0, 2), (2, 0), (1, 1), (1, 3), (3, 1), (3, 3),
               (2, 1), (1, 2), (2, 3), (3, 2), (2, 2)]
slot_at = {group: index for index, group in enumerate(group_order)}
arrivals = [
    [],
    [(0, 1, 0), (0, 3, 0), (1, 0, 0), (3, 0, 0), (0, 1, 1), (0, 3, 1), (1, 0, 1), (3, 0, 1)],
    [], [],
    [(1, 1, 0), (0, 2, 0), (2, 0, 0)],
    [(2, 0, 1), (1, 3, 0), (3, 1, 0), (0, 2, 1), (3, 3, 0)],
    [(1, 1, 1), (1, 3, 1)],
    [(3, 1, 1)],
    [(3, 3, 1)],
    [(2, 1, 0)],
    [(2, 3, 0)],
    [(2, 1, 1), (2, 3, 1), (1, 2, 0), (1, 2, 1)],
    [],
    [(3, 2, 0), (3, 2, 1)],
    [],
    [(2, 2, 0), (2, 2, 1)],
]
links = [(1, 0), (3, 0), (0, 1), (0, 3)]


def onward(da, db, part):
    first_half = part < pieces // 2
    taken = []
    if db == 0:
        if da == 0 or (da == 3 and first_half):
            taken.append(0)
        if da == 0 or (da == 1 and not first_half):
            taken.append(1)
        taken += [2, 3]
    else:
        if db == 3 and first_half:
            taken.append(2)
        if db == 1 and not first_half:
            taken.append(3)
    return taken


send_count = 0
send_plan = {}
for arrival_group in group_order:
    for arrival_part in range(pieces):
        for link_taken in ["partner"] + onward(*arrival_group, arrival_part):
            send_plan[(arrival_group, arrival_part, link_taken)] = send_count
            send_count += 1


def kernel(lens, slots, hidden, gain, targets, weight_hbm, out_logprob, out_entropy,
           weight, weight_t, rows, tags, tag_out, own_stats, stats_in, fin, gathered,
           weight_sem, send_sem, arrive_sem, partner_sem, tag_send, tag_recv,
           stat_send, stat_recv, z_send, z_recv, fin_send, fin_recv):
    req = lax.axis_index("req")
    me = lax.axis_index("vocab")
    core = lax.rem(me, 2)
    chip_x = lax.rem(me // 2, side)
    chip_y = me // (2 * side)
    members = 2 * side * side
    columns = weight.shape[1]

    def device_at(da, db, other):
        x = lax.rem(chip_x + da * (1 - core) + db * core, side)
        y = lax.rem(chip_y + db * (1 - core) + da * core, side)
        the_core = (1 - core) if other else core
        return (y * side + x) * 2 + the_core

    barrier = pltpu.get_barrier_semaphore()

    def greet(step, carry):
        pl.semaphore_signal(barrier, inc=1, device_id=(req, lax.rem(me + step, members)), device_id_type=mesh_ids)
        return carry

    lax.fori_loop(1, members, greet, 0)
    for step in range(1, side):
        pl.semaphore_signal(barrier, inc=1, device_id=(lax.rem(req + step, side), me), device_id_type=mesh_ids)

    weight_copy = pltpu.make_async_copy(weight_hbm, weight, weight_sem)
    weight_copy.start()

    seq_count = lens.shape[0]
    held = hidden.shape[0]
    seq_len = held // seq_count
    offsets = []
    running = jnp.int32(0)
    for seq in range(seq_count):
        offsets.append(running)
        running = running + lens[seq]

    def compact_place(slot_index):
        place = jnp.full(slot_index.shape, -1, jnp.int32)
        for seq in range(seq_count):
            ahead = slot_index - seq * seq_len
            place = jnp.where((ahead >= 0) & (ahead < lens[seq]), ahead + offsets[seq], place)
        return place

    place_row = compact_place(lax.broadcasted_iota(jnp.int32, (8, held), 1))[:1]
    pick = (lax.broadcasted_iota(jnp.int32, (cap, held), 0) == place_row).astype(f32).astype(jnp.bfloat16)
    live = jnp.dot(pick, hidden[...], preferred_element_type=f32)
    inverse_rms = lax.rsqrt(jnp.mean(live * live, axis=1, keepdims=True) + eps_norm)
    rows[0, 0:cap, :] = (live * inverse_rms * gain[...]).astype(jnp.bfloat16)

    place_col = compact_place(lax.broadcasted_iota(jnp.int32, (held, cap), 0))
    pick_t = (lax.broadcasted_iota(jnp.int32, (held, cap), 1) == place_col).astype(f32).astype(jnp.bfloat16)
    wide = targets[...]
    high = wide // 256
    digits = jnp.concatenate([high, wide - high * 256] + [jnp.zeros_like(wide)] * 14, axis=0)
    digits = digits.astype(f32).astype(jnp.bfloat16)
    tag_pair = jnp.dot(digits, pick_t, preferred_element_type=f32)
    tag_own = (tag_pair[0:1] * 256.0 + tag_pair[1:2]).astype(jnp.int32)
    tag_out[0] = tag_own
    tags[me] = tag_own

    pl.semaphore_wait(barrier, members - 1 + side - 1)

    def piece_copy(group, part, link):
        da, db = group
        source = rows.at[slot_at[group], pl.ds(part * piece_rows, piece_rows), :]
        if link == "partner":
            return pltpu.make_async_remote_copy(
                src_ref=source,
                dst_ref=rows.at[slot_at[(db, da)], pl.ds(cap + part * piece_rows, piece_rows), :],
                send_sem=send_sem.at[send_plan[(group, part, link)]],
                recv_sem=partner_sem.at[slot_at[(db, da)] * pieces + part],
                device_id=(req, device_at(0, 0, True)), device_id_type=mesh_ids)
        ma, mb = links[link]
        landing = slot_at[((da - ma) % side, (db - mb) % side)]
        return pltpu.make_async_remote_copy(
            src_ref=source,
            dst_ref=rows.at[landing, pl.ds(part * piece_rows, piece_rows), :],
            send_sem=send_sem.at[send_plan[(group, part, link)]],
            recv_sem=arrive_sem.at[landing * pieces + part],
            device_id=(req, device_at(ma, mb, False)), device_id_type=mesh_ids)

    def arrived(slot, part):
        here = rows.at[slot, pl.ds(part * piece_rows, piece_rows), :]
        return pltpu.make_async_copy(here, here, arrive_sem.at[slot * pieces + part])

    def send_onward(da, db, part):
        for link in onward(da, db, part):
            piece_copy((da, db), part, link).start()
        piece_copy((da, db), part, "partner").start()

    for part in range(pieces):
        send_onward(0, 0, part)

    def tag_copy(step):
        return pltpu.make_async_remote_copy(
            src_ref=tag_out.at[0], dst_ref=tags.at[me], send_sem=tag_send, recv_sem=tag_recv,
            device_id=(req, lax.rem(me + step, members)), device_id_type=mesh_ids)

    def send_tag(step, carry):
        tag_copy(step).start()
        return carry

    lax.fori_loop(1, members, send_tag, 0)

    weight_copy.wait()
    depth = weight.shape[0]
    chunk = 256

    def turn(step, carry):
        start = pl.multiple_of(step * chunk, chunk)
        weight_t[:, pl.ds(start, chunk)] = weight[pl.ds(start, chunk), :].T
        return carry

    lax.fori_loop(0, depth // chunk, turn, 0)

    pltpu.make_async_copy(tags.at[pl.ds(0, members - 1)], tags.at[pl.ds(0, members - 1)], tag_recv).wait()

    def stat_copy(group, other):
        owner = device_at(group[0], group[1], other)
        index = slot_at[group] * 2 + other
        return pltpu.make_async_remote_copy(
            src_ref=own_stats.at[slot_at[group], other], dst_ref=stats_in.at[me],
            send_sem=stat_send.at[index], recv_sem=stat_recv,
            device_id=(req, owner), device_id_type=mesh_ids)

    first_column = me * columns

    def one_group(step, carry):
        for index in range(len(group_order)):
            if arrivals[index]:
                @pl.when(step == index)
                def _():
                    for da, db, part in arrivals[index]:
                        arrived(slot_at[(da, db)], part).wait()
                        send_onward(da, db, part)

        for part in range(pieces):
            there = rows.at[step, pl.ds(cap + part * piece_rows, piece_rows), :]
            pltpu.make_async_copy(there, there, partner_sem.at[step * pieces + part]).wait()

        logits = lax.dot_general(weight_t[...], rows[step], (((1,), (1,)), ((), ())), preferred_element_type=f32)
        da = jnp.int32(0)
        db = jnp.int32(0)
        for index, group in enumerate(group_order):
            da = jnp.where(step == index, group[0], da)
            db = jnp.where(step == index, group[1], db)
        for other in range(2):
            part_logits = logits[:, other * cap:(other + 1) * cap]
            tag = tags[device_at(da, db, other)] - first_column
            peak = jnp.max(part_logits, axis=0, keepdims=True)
            shifted = part_logits - peak
            exponent = jnp.exp(shifted)
            total = jnp.sum(exponent, axis=0, keepdims=True)
            spread = jnp.sum(exponent * shifted, axis=0, keepdims=True)
            column = lax.broadcasted_iota(jnp.int32, part_logits.shape, 0)
            picked = jnp.sum(jnp.where(column == tag, part_logits, 0.0), axis=0, keepdims=True)
            own_stats[step, other] = jnp.concatenate([peak, total, spread, picked] * 2, axis=0)

        for index, group in enumerate(group_order):
            @pl.when(step == index)
            def _():
                for other in range(2):
                    if index == 0 and other == 0:
                        stats_in[me] = own_stats[0, 0]
                    else:
                        stat_copy(group, other).start()
        return carry

    lax.fori_loop(0, len(group_order), one_group, 0)

    pltpu.make_async_copy(stats_in.at[pl.ds(0, members - 1)], stats_in.at[pl.ds(0, members - 1)], stat_recv).wait()

    peak = stats_in[0]
    for index in range(1, members):
        peak = jnp.maximum(peak, stats_in[index])
    peak = peak[0:1]
    row_total = jnp.zeros((1, cap), f32)
    spread = jnp.zeros((1, cap), f32)
    picked = jnp.zeros((1, cap), f32)
    for index in range(members):
        tile = stats_in[index]
        below = tile[0:1] - peak
        factor = jnp.exp(below)
        row_total = row_total + tile[1:2] * factor
        spread = spread + factor * (tile[2:3] + below * tile[1:2])
        picked = picked + tile[3:4]
    log_total = jnp.log(row_total)
    logprob = jnp.broadcast_to(picked - peak - log_total, (seq_count, cap))
    entropy = jnp.broadcast_to(log_total - spread / row_total, (seq_count, cap))

    request = lax.broadcasted_iota(jnp.int32, (seq_count, cap), 0)
    lane = lax.broadcasted_iota(jnp.int32, (seq_count, cap), 1)
    offset = jnp.zeros((seq_count, cap), jnp.int32)
    length = jnp.zeros((seq_count, cap), jnp.int32)
    for seq in range(seq_count):
        offset = jnp.where(request == seq, offsets[seq], offset)
        length = jnp.where(request == seq, lens[seq], length)
    bit = 1
    while bit < cap:
        moved = (offset & bit) != 0
        logprob = jnp.where(moved, pltpu.roll(logprob, cap - bit, 1), logprob)
        entropy = jnp.where(moved, pltpu.roll(entropy, cap - bit, 1), entropy)
        bit *= 2
    logprob = jnp.where(lane < length, logprob, 0.0)
    entropy = jnp.where(lane < length, entropy, 0.0)
    both = logprob + pltpu.roll(entropy, seq_len, 1)
    half = seq_count // 2
    fin[me, req] = both[:half] + pltpu.roll(both[half:], cap // 2, 1)

    def z_copy(step):
        return pltpu.make_async_remote_copy(
            src_ref=fin.at[me, req], dst_ref=fin.at[me, req], send_sem=z_send.at[step - 1], recv_sem=z_recv,
            device_id=(lax.rem(req + step, side), me), device_id_type=mesh_ids)

    for step in range(1, side):
        z_copy(step).start()
    pltpu.make_async_copy(fin.at[me, pl.ds(0, side - 1)], fin.at[me, pl.ds(0, side - 1)], z_recv).wait()

    def fin_copy(step):
        return pltpu.make_async_remote_copy(
            src_ref=fin.at[me], dst_ref=fin.at[me], send_sem=fin_send, recv_sem=fin_recv,
            device_id=(req, lax.rem(me + step, members)), device_id_type=mesh_ids)

    def send_fin(step, carry):
        fin_copy(step).start()
        return carry

    lax.fori_loop(1, members, send_fin, 0)
    pltpu.make_async_copy(fin.at[pl.ds(0, members - 1)], fin.at[pl.ds(0, members - 1)], fin_recv).wait()

    for seq in range(seq_count):
        wanted = slots[seq]
        owner = lax.div(wanted, seq_count)
        inside = lax.rem(wanted, seq_count)
        tile = fin[lax.rem(owner, members), lax.div(owner, members)]
        turned = pltpu.roll(tile, cap // 2, 1)
        tile = jnp.where(inside >= half, turned, tile)
        level = lax.rem(inside, half)
        row = lax.broadcasted_iota(jnp.int32, (half, cap), 0)
        gathered[pl.ds(seq, 1), :] = jnp.sum(jnp.where(row == level, tile, 0.0), axis=0, keepdims=True)
    out_logprob[...] = gathered[:, 0:seq_len]
    out_entropy[...] = gathered[:, seq_len:2 * seq_len]

    def drain(index, carry):
        here = rows.at[0, pl.ds(0, piece_rows), :]
        pltpu.make_async_copy(here, here, send_sem.at[index]).wait()
        return carry

    lax.fori_loop(0, send_count, drain, 0)
    pltpu.make_async_copy(tags.at[pl.ds(0, members - 1)], tags.at[pl.ds(0, members - 1)], tag_send).wait()

    def drain_stats(index, carry):
        pltpu.make_async_copy(stats_in.at[0], stats_in.at[0], stat_send.at[index]).wait()
        return carry

    lax.fori_loop(1, 2 * len(group_order), drain_stats, 0)
    for step in range(1, side):
        z_copy(step).wait_send()
    pltpu.make_async_copy(fin.at[pl.ds(0, members - 1)], fin.at[pl.ds(0, members - 1)], fin_send).wait()


def local(hidden_states, norm_gain, head_weight, targets, lengths, slot_of):
    held, depth = hidden_states.shape
    seq_count = lengths.shape[0]
    seq_len = held // seq_count
    columns = head_weight.shape[1]
    groups = side * side
    members = 2 * groups
    vmem = pl.BlockSpec(memory_space=pltpu.VMEM)
    smem = pl.BlockSpec(memory_space=pltpu.SMEM)
    dma = pltpu.SemaphoreType.DMA
    out = jax.ShapeDtypeStruct((seq_count, seq_len), f32)
    return pl.pallas_call(
        kernel,
        out_shape=(out, out),
        in_specs=[smem, smem, vmem, vmem, vmem, pl.BlockSpec(memory_space=pl.ANY)],
        out_specs=(vmem, vmem),
        scratch_shapes=[
            pltpu.VMEM((depth, columns), jnp.bfloat16),
            pltpu.VMEM((columns, depth), jnp.bfloat16),
            pltpu.VMEM((groups, 2 * cap, depth), jnp.bfloat16),
            pltpu.VMEM((members, 1, cap), jnp.int32),
            pltpu.VMEM((1, 1, cap), jnp.int32),
            pltpu.VMEM((groups, 2, 8, cap), f32),
            pltpu.VMEM((members, 8, cap), f32),
            pltpu.VMEM((members, side, seq_count // 2, cap), f32),
            pltpu.VMEM((seq_count, cap), f32),
            dma,
            dma((send_count,)),
            dma((groups * pieces,)),
            dma((groups * pieces,)),
            dma, dma,
            dma((members,)),
            dma,
            dma((side - 1,)),
            dma, dma, dma,
        ],
        compiler_params=pltpu.CompilerParams(collective_id=0, has_side_effects=True, vmem_limit_bytes=60 << 20),
        name="head_stats",
    )(lengths, slot_of, hidden_states, norm_gain.reshape(1, depth), targets.reshape(1, held), head_weight)


def solution(mesh):
    rows = jax.sharding.PartitionSpec(("req", "vocab"), None)
    flat = jax.sharding.PartitionSpec(("req", "vocab"))
    in_specs = (rows, jax.sharding.PartitionSpec(), jax.sharding.PartitionSpec(None, "vocab"), flat, flat, flat)
    return jax.shard_map(local, mesh=mesh, in_specs=in_specs, out_specs=(rows, rows), check_vma=False)
```

```python
import jax
import jax.numpy as jnp
from jax import lax
from jax.experimental import pallas as pl
from jax.experimental.pallas import tpu as pltpu

eps_norm = 1e-05
side = 4
cap = 128
pieces = 2
piece_rows = cap // pieces
mesh_ids = pl.DeviceIdType.MESH
f32 = jnp.float32

group_order = [(0, 0), (0, 1), (1, 0), (0, 3), (3, 0), (0, 2), (2, 0), (1, 1), (1, 3), (3, 1), (3, 3),
               (2, 1), (1, 2), (2, 3), (3, 2), (2, 2)]
slot_at = {group: index for index, group in enumerate(group_order)}
arrivals = [
    [],
    [(0, 1, 0), (0, 3, 0), (1, 0, 0), (3, 0, 0), (0, 1, 1), (0, 3, 1), (1, 0, 1), (3, 0, 1)],
    [], [],
    [(1, 1, 0), (0, 2, 0), (2, 0, 0)],
    [(2, 0, 1), (1, 3, 0), (3, 1, 0), (0, 2, 1), (3, 3, 0)],
    [(1, 1, 1), (1, 3, 1)],
    [(3, 1, 1)],
    [(3, 3, 1)],
    [(2, 1, 0)],
    [(2, 3, 0)],
    [(2, 1, 1), (2, 3, 1), (1, 2, 0), (1, 2, 1)],
    [],
    [(3, 2, 0), (3, 2, 1)],
    [],
    [(2, 2, 0), (2, 2, 1)],
]
links = [(1, 0), (3, 0), (0, 1), (0, 3)]


def onward(da, db, part):
    first_half = part < pieces // 2
    taken = []
    if db == 0:
        if da == 0 or (da == 3 and first_half):
            taken.append(0)
        if da == 0 or (da == 1 and not first_half):
            taken.append(1)
        taken += [2, 3]
    else:
        if db == 3 and first_half:
            taken.append(2)
        if db == 1 and not first_half:
            taken.append(3)
    return taken


send_count = 0
send_plan = {}
for arrival_group in group_order:
    for arrival_part in range(pieces):
        for link_taken in ["partner"] + onward(*arrival_group, arrival_part):
            send_plan[(arrival_group, arrival_part, link_taken)] = send_count
            send_count += 1


def kernel(lens, slots, hidden, gain, targets, weight_hbm, out_logprob, out_entropy,
           weight_t, rows, tags, tag_out, own_stats, stats_in, fin, gathered,
           weight_sem, send_sem, arrive_sem, partner_sem, tag_send, tag_recv,
           stat_send, stat_recv, z_send, z_recv, fin_send, fin_recv):
    req = lax.axis_index("req")
    me = lax.axis_index("vocab")
    core = lax.rem(me, 2)
    chip_x = lax.rem(me // 2, side)
    chip_y = me // (2 * side)
    members = 2 * side * side
    columns, depth = weight_t.shape

    def device_at(da, db, other):
        x = lax.rem(chip_x + da * (1 - core) + db * core, side)
        y = lax.rem(chip_y + db * (1 - core) + da * core, side)
        the_core = (1 - core) if other else core
        return (y * side + x) * 2 + the_core

    barrier = pltpu.get_barrier_semaphore()

    def greet(step, carry):
        pl.semaphore_signal(barrier, inc=1, device_id=(req, lax.rem(me + step, members)), device_id_type=mesh_ids)
        return carry

    lax.fori_loop(1, members, greet, 0)
    for step in range(1, side):
        pl.semaphore_signal(barrier, inc=1, device_id=(lax.rem(req + step, side), me), device_id_type=mesh_ids)

    weight_copy = pltpu.make_async_copy(weight_hbm, weight_t, weight_sem)
    weight_copy.start()

    seq_count = lens.shape[0]
    held = hidden.shape[0]
    seq_len = held // seq_count
    offsets = []
    running = jnp.int32(0)
    for seq in range(seq_count):
        offsets.append(running)
        running = running + lens[seq]

    def compact_place(slot_index):
        place = jnp.full(slot_index.shape, -1, jnp.int32)
        for seq in range(seq_count):
            ahead = slot_index - seq * seq_len
            place = jnp.where((ahead >= 0) & (ahead < lens[seq]), ahead + offsets[seq], place)
        return place

    place_row = compact_place(lax.broadcasted_iota(jnp.int32, (8, held), 1))[:1]
    pick = (lax.broadcasted_iota(jnp.int32, (cap, held), 0) == place_row).astype(f32).astype(jnp.bfloat16)
    live = jnp.dot(pick, hidden[...], preferred_element_type=f32)
    inverse_rms = lax.rsqrt(jnp.mean(live * live, axis=1, keepdims=True) + eps_norm)
    rows[0, 0:cap, :] = (live * inverse_rms * gain[...]).astype(jnp.bfloat16)

    place_col = compact_place(lax.broadcasted_iota(jnp.int32, (held, cap), 0))
    pick_t = (lax.broadcasted_iota(jnp.int32, (held, cap), 1) == place_col).astype(f32).astype(jnp.bfloat16)
    wide = targets[...]
    high = wide // 256
    digits = jnp.concatenate([high, wide - high * 256] + [jnp.zeros_like(wide)] * 14, axis=0)
    digits = digits.astype(f32).astype(jnp.bfloat16)
    tag_pair = jnp.dot(digits, pick_t, preferred_element_type=f32)
    tag_own = (tag_pair[0:1] * 256.0 + tag_pair[1:2]).astype(jnp.int32)
    tag_out[0] = tag_own
    tags[me] = tag_own

    pl.semaphore_wait(barrier, members - 1 + side - 1)

    def piece_copy(group, part, link):
        da, db = group
        source = rows.at[slot_at[group], pl.ds(part * piece_rows, piece_rows), :]
        if link == "partner":
            return pltpu.make_async_remote_copy(
                src_ref=source,
                dst_ref=rows.at[slot_at[(db, da)], pl.ds(cap + part * piece_rows, piece_rows), :],
                send_sem=send_sem.at[send_plan[(group, part, link)]],
                recv_sem=partner_sem.at[slot_at[(db, da)] * pieces + part],
                device_id=(req, device_at(0, 0, True)), device_id_type=mesh_ids)
        ma, mb = links[link]
        landing = slot_at[((da - ma) % side, (db - mb) % side)]
        return pltpu.make_async_remote_copy(
            src_ref=source,
            dst_ref=rows.at[landing, pl.ds(part * piece_rows, piece_rows), :],
            send_sem=send_sem.at[send_plan[(group, part, link)]],
            recv_sem=arrive_sem.at[landing * pieces + part],
            device_id=(req, device_at(ma, mb, False)), device_id_type=mesh_ids)

    def arrived(slot, part):
        here = rows.at[slot, pl.ds(part * piece_rows, piece_rows), :]
        return pltpu.make_async_copy(here, here, arrive_sem.at[slot * pieces + part])

    def send_onward(da, db, part):
        for link in onward(da, db, part):
            piece_copy((da, db), part, link).start()
        piece_copy((da, db), part, "partner").start()

    for part in range(pieces):
        send_onward(0, 0, part)

    def tag_copy(step):
        return pltpu.make_async_remote_copy(
            src_ref=tag_out.at[0], dst_ref=tags.at[me], send_sem=tag_send, recv_sem=tag_recv,
            device_id=(req, lax.rem(me + step, members)), device_id_type=mesh_ids)

    def send_tag(step, carry):
        tag_copy(step).start()
        return carry

    lax.fori_loop(1, members, send_tag, 0)

    weight_copy.wait()
    pltpu.make_async_copy(tags.at[pl.ds(0, members - 1)], tags.at[pl.ds(0, members - 1)], tag_recv).wait()

    def stat_copy(group, other):
        owner = device_at(group[0], group[1], other)
        index = slot_at[group] * 2 + other
        return pltpu.make_async_remote_copy(
            src_ref=own_stats.at[slot_at[group], other], dst_ref=stats_in.at[me],
            send_sem=stat_send.at[index], recv_sem=stat_recv,
            device_id=(req, owner), device_id_type=mesh_ids)

    first_column = me * columns

    def one_group(step, carry):
        for index in range(len(group_order)):
            if arrivals[index]:
                @pl.when(step == index)
                def _():
                    for da, db, part in arrivals[index]:
                        arrived(slot_at[(da, db)], part).wait()
                        send_onward(da, db, part)

        for part in range(pieces):
            there = rows.at[step, pl.ds(cap + part * piece_rows, piece_rows), :]
            pltpu.make_async_copy(there, there, partner_sem.at[step * pieces + part]).wait()

        logits = lax.dot_general(weight_t[...], rows[step], (((1,), (1,)), ((), ())), preferred_element_type=f32)
        da = jnp.int32(0)
        db = jnp.int32(0)
        for index, group in enumerate(group_order):
            da = jnp.where(step == index, group[0], da)
            db = jnp.where(step == index, group[1], db)
        for other in range(2):
            part_logits = logits[:, other * cap:(other + 1) * cap]
            tag = tags[device_at(da, db, other)] - first_column
            peak = jnp.max(part_logits, axis=0, keepdims=True)
            shifted = part_logits - peak
            exponent = jnp.exp(shifted)
            total = jnp.sum(exponent, axis=0, keepdims=True)
            spread = jnp.sum(exponent * shifted, axis=0, keepdims=True)
            column = lax.broadcasted_iota(jnp.int32, part_logits.shape, 0)
            picked = jnp.sum(jnp.where(column == tag, part_logits, 0.0), axis=0, keepdims=True)
            own_stats[step, other] = jnp.concatenate([peak, total, spread, picked] * 2, axis=0)

        for index, group in enumerate(group_order):
            @pl.when(step == index)
            def _():
                for other in range(2):
                    if index == 0 and other == 0:
                        stats_in[me] = own_stats[0, 0]
                    else:
                        stat_copy(group, other).start()
        return carry

    lax.fori_loop(0, len(group_order), one_group, 0)

    pltpu.make_async_copy(stats_in.at[pl.ds(0, members - 1)], stats_in.at[pl.ds(0, members - 1)], stat_recv).wait()

    peak = stats_in[0]
    for index in range(1, members):
        peak = jnp.maximum(peak, stats_in[index])
    peak = peak[0:1]
    row_total = jnp.zeros((1, cap), f32)
    spread = jnp.zeros((1, cap), f32)
    picked = jnp.zeros((1, cap), f32)
    for index in range(members):
        tile = stats_in[index]
        below = tile[0:1] - peak
        factor = jnp.exp(below)
        row_total = row_total + tile[1:2] * factor
        spread = spread + factor * (tile[2:3] + below * tile[1:2])
        picked = picked + tile[3:4]
    log_total = jnp.log(row_total)
    logprob = jnp.broadcast_to(picked - peak - log_total, (seq_count, cap))
    entropy = jnp.broadcast_to(log_total - spread / row_total, (seq_count, cap))

    request = lax.broadcasted_iota(jnp.int32, (seq_count, cap), 0)
    lane = lax.broadcasted_iota(jnp.int32, (seq_count, cap), 1)
    offset = jnp.zeros((seq_count, cap), jnp.int32)
    length = jnp.zeros((seq_count, cap), jnp.int32)
    for seq in range(seq_count):
        offset = jnp.where(request == seq, offsets[seq], offset)
        length = jnp.where(request == seq, lens[seq], length)
    bit = 1
    while bit < cap:
        moved = (offset & bit) != 0
        logprob = jnp.where(moved, pltpu.roll(logprob, cap - bit, 1), logprob)
        entropy = jnp.where(moved, pltpu.roll(entropy, cap - bit, 1), entropy)
        bit *= 2
    logprob = jnp.where(lane < length, logprob, 0.0)
    entropy = jnp.where(lane < length, entropy, 0.0)
    both = logprob + pltpu.roll(entropy, seq_len, 1)
    half = seq_count // 2
    fin[me, req] = both[:half] + pltpu.roll(both[half:], cap // 2, 1)

    def z_copy(step):
        return pltpu.make_async_remote_copy(
            src_ref=fin.at[me, req], dst_ref=fin.at[me, req], send_sem=z_send.at[step - 1], recv_sem=z_recv,
            device_id=(lax.rem(req + step, side), me), device_id_type=mesh_ids)

    for step in range(1, side):
        z_copy(step).start()
    pltpu.make_async_copy(fin.at[me, pl.ds(0, side - 1)], fin.at[me, pl.ds(0, side - 1)], z_recv).wait()

    def fin_copy(step):
        return pltpu.make_async_remote_copy(
            src_ref=fin.at[me], dst_ref=fin.at[me], send_sem=fin_send, recv_sem=fin_recv,
            device_id=(req, lax.rem(me + step, members)), device_id_type=mesh_ids)

    def send_fin(step, carry):
        fin_copy(step).start()
        return carry

    lax.fori_loop(1, members, send_fin, 0)
    pltpu.make_async_copy(fin.at[pl.ds(0, members - 1)], fin.at[pl.ds(0, members - 1)], fin_recv).wait()

    for seq in range(seq_count):
        wanted = slots[seq]
        owner = lax.div(wanted, seq_count)
        inside = lax.rem(wanted, seq_count)
        tile = fin[lax.rem(owner, members), lax.div(owner, members)]
        turned = pltpu.roll(tile, cap // 2, 1)
        tile = jnp.where(inside >= half, turned, tile)
        level = lax.rem(inside, half)
        row = lax.broadcasted_iota(jnp.int32, (half, cap), 0)
        gathered[pl.ds(seq, 1), :] = jnp.sum(jnp.where(row == level, tile, 0.0), axis=0, keepdims=True)
    out_logprob[...] = gathered[:, 0:seq_len]
    out_entropy[...] = gathered[:, seq_len:2 * seq_len]

    def drain(index, carry):
        here = rows.at[0, pl.ds(0, piece_rows), :]
        pltpu.make_async_copy(here, here, send_sem.at[index]).wait()
        return carry

    lax.fori_loop(0, send_count, drain, 0)
    pltpu.make_async_copy(tags.at[pl.ds(0, members - 1)], tags.at[pl.ds(0, members - 1)], tag_send).wait()

    def drain_stats(index, carry):
        pltpu.make_async_copy(stats_in.at[0], stats_in.at[0], stat_send.at[index]).wait()
        return carry

    lax.fori_loop(1, 2 * len(group_order), drain_stats, 0)
    for step in range(1, side):
        z_copy(step).wait_send()
    pltpu.make_async_copy(fin.at[pl.ds(0, members - 1)], fin.at[pl.ds(0, members - 1)], fin_send).wait()


def local(hidden_states, norm_gain, head_weight, targets, lengths, slot_of):
    held, depth = hidden_states.shape
    seq_count = lengths.shape[0]
    seq_len = held // seq_count
    columns = head_weight.shape[1]
    groups = side * side
    members = 2 * groups
    vmem = pl.BlockSpec(memory_space=pltpu.VMEM)
    smem = pl.BlockSpec(memory_space=pltpu.SMEM)
    dma = pltpu.SemaphoreType.DMA
    out = jax.ShapeDtypeStruct((seq_count, seq_len), f32)
    return pl.pallas_call(
        kernel,
        out_shape=(out, out),
        in_specs=[smem, smem, vmem, vmem, vmem, pl.BlockSpec(memory_space=pl.ANY)],
        out_specs=(vmem, vmem),
        scratch_shapes=[
            pltpu.VMEM((columns, depth), jnp.bfloat16),
            pltpu.VMEM((groups, 2 * cap, depth), jnp.bfloat16),
            pltpu.VMEM((members, 1, cap), jnp.int32),
            pltpu.VMEM((1, 1, cap), jnp.int32),
            pltpu.VMEM((groups, 2, 8, cap), f32),
            pltpu.VMEM((members, 8, cap), f32),
            pltpu.VMEM((members, side, seq_count // 2, cap), f32),
            pltpu.VMEM((seq_count, cap), f32),
            dma,
            dma((send_count,)),
            dma((groups * pieces,)),
            dma((groups * pieces,)),
            dma, dma,
            dma((members,)),
            dma,
            dma((side - 1,)),
            dma, dma, dma,
        ],
        compiler_params=pltpu.CompilerParams(collective_id=0, has_side_effects=True, vmem_limit_bytes=60 << 20),
        name="head_stats",
    )(lengths, slot_of, hidden_states, norm_gain.reshape(1, depth), targets.reshape(1, held), head_weight.T)


def solution(mesh):
    rows = jax.sharding.PartitionSpec(("req", "vocab"), None)
    flat = jax.sharding.PartitionSpec(("req", "vocab"))
    in_specs = (rows, jax.sharding.PartitionSpec(), jax.sharding.PartitionSpec(None, "vocab"), flat, flat, flat)
    return jax.shard_map(local, mesh=mesh, in_specs=in_specs, out_specs=(rows, rows), check_vma=False)
```

```python
import jax
import jax.numpy as jnp
from jax import lax
from jax.experimental import pallas as pl
from jax.experimental.pallas import tpu as pltpu

eps_norm = 1e-05
side = 4
cap = 128
pieces = 2
piece_rows = cap // pieces
mesh_ids = pl.DeviceIdType.MESH
f32 = jnp.float32

group_order = [(0, 0), (0, 1), (1, 0), (0, 3), (3, 0), (0, 2), (2, 0), (1, 1), (1, 3), (3, 1), (3, 3),
               (2, 1), (1, 2), (2, 3), (3, 2), (2, 2)]
slot_at = {group: index for index, group in enumerate(group_order)}
arrivals = [
    [],
    [(0, 1, 0), (0, 3, 0), (1, 0, 0), (3, 0, 0), (0, 1, 1), (0, 3, 1), (1, 0, 1), (3, 0, 1)],
    [], [],
    [(1, 1, 0), (0, 2, 0), (2, 0, 0)],
    [(2, 0, 1), (1, 3, 0), (3, 1, 0), (0, 2, 1), (3, 3, 0)],
    [(1, 1, 1), (1, 3, 1)],
    [(3, 1, 1)],
    [(3, 3, 1)],
    [(2, 1, 0)],
    [(2, 3, 0)],
    [(2, 1, 1), (2, 3, 1), (1, 2, 0), (1, 2, 1)],
    [],
    [(3, 2, 0), (3, 2, 1)],
    [],
    [(2, 2, 0), (2, 2, 1)],
]
links = [(1, 0), (3, 0), (0, 1), (0, 3)]


def onward(da, db, part):
    first_half = part < pieces // 2
    taken = []
    if db == 0:
        if da == 0 or (da == 3 and first_half):
            taken.append(0)
        if da == 0 or (da == 1 and not first_half):
            taken.append(1)
        taken += [2, 3]
    else:
        if db == 3 and first_half:
            taken.append(2)
        if db == 1 and not first_half:
            taken.append(3)
    return taken


def tag_part(group, link):
    if link == "partner":
        return 0
    carried = [part for part in range(pieces) if link in onward(*group, part)]
    return carried[0] if carried else None


tag_plan = {}
for tag_group in group_order:
    for tag_link in ["partner"] + list(range(4)):
        if tag_part(tag_group, tag_link) == 0:
            tag_plan[(tag_group, tag_link)] = len(tag_plan)

send_count = 0
send_plan = {}
for arrival_group in group_order:
    for arrival_part in range(pieces):
        for link_taken in ["partner"] + onward(*arrival_group, arrival_part):
            send_plan[(arrival_group, arrival_part, link_taken)] = send_count
            send_count += 1


def kernel(lens, slots, hidden, gain, targets, weight_hbm, out,
           weight_t, rows, tags, own_stats, stats_in, fin, gathered,
           weight_sem, send_sem, arrive_sem, partner_sem, tag_send, tag_recv,
           stat_send, stat_recv, token, fin_send, fin_recv):
    req = lax.axis_index("req")
    me = lax.axis_index("vocab")
    core = lax.rem(me, 2)
    chip_x = lax.rem(me // 2, side)
    chip_y = me // (2 * side)
    members = 2 * side * side
    columns, depth = weight_t.shape

    def device_at(da, db, other):
        x = lax.rem(chip_x + da * (1 - core) + db * core, side)
        y = lax.rem(chip_y + db * (1 - core) + da * core, side)
        the_core = (1 - core) if other else core
        return (y * side + x) * 2 + the_core

    barrier = pltpu.get_barrier_semaphore()

    neighbours = [(1, 0, False), (3, 0, False), (0, 1, False), (0, 3, False), (0, 0, True)]
    for neighbour in neighbours:
        pl.semaphore_signal(barrier, inc=1, device_id=(req, device_at(*neighbour)), device_id_type=mesh_ids)
    for step in range(1, side):
        pl.semaphore_signal(barrier, inc=1, device_id=(lax.rem(req + step, side), me), device_id_type=mesh_ids)

    weight_copy = pltpu.make_async_copy(weight_hbm, weight_t, weight_sem)
    weight_copy.start()

    seq_count = lens.shape[0]
    held = hidden.shape[0]
    seq_len = held // seq_count
    offsets = []
    running = jnp.int32(0)
    for seq in range(seq_count):
        offsets.append(running)
        running = running + lens[seq]

    def compact_place(slot_index):
        place = jnp.full(slot_index.shape, -1, jnp.int32)
        for seq in range(seq_count):
            ahead = slot_index - seq * seq_len
            place = jnp.where((ahead >= 0) & (ahead < lens[seq]), ahead + offsets[seq], place)
        return place

    place_row = compact_place(lax.broadcasted_iota(jnp.int32, (8, held), 1))[:1]
    pick = (lax.broadcasted_iota(jnp.int32, (cap, held), 0) == place_row).astype(f32).astype(jnp.bfloat16)
    live = jnp.dot(pick, hidden[...], preferred_element_type=f32)
    inverse_rms = lax.rsqrt(jnp.mean(live * live, axis=1, keepdims=True) + eps_norm)
    rows[0, 0:cap, :] = (live * inverse_rms * gain[...]).astype(jnp.bfloat16)

    place_col = compact_place(lax.broadcasted_iota(jnp.int32, (held, cap), 0))
    pick_t = (lax.broadcasted_iota(jnp.int32, (held, cap), 1) == place_col).astype(f32).astype(jnp.bfloat16)
    wide = targets[...]
    high = wide // 256
    digits = jnp.concatenate([high, wide - high * 256] + [jnp.zeros_like(wide)] * 14, axis=0)
    digits = digits.astype(f32).astype(jnp.bfloat16)
    tag_pair = jnp.dot(digits, pick_t, preferred_element_type=f32)
    tag_own = (tag_pair[0:1] * 256.0 + tag_pair[1:2]).astype(jnp.int32)
    tags[0] = tag_own

    pl.semaphore_wait(barrier, len(neighbours) + side - 1)

    def piece_copy(group, part, link):
        da, db = group
        source = rows.at[slot_at[group], pl.ds(part * piece_rows, piece_rows), :]
        if link == "partner":
            return pltpu.make_async_remote_copy(
                src_ref=source,
                dst_ref=rows.at[slot_at[(db, da)], pl.ds(cap + part * piece_rows, piece_rows), :],
                send_sem=send_sem.at[send_plan[(group, part, link)]],
                recv_sem=partner_sem.at[slot_at[(db, da)] * pieces + part],
                device_id=(req, device_at(0, 0, True)), device_id_type=mesh_ids)
        ma, mb = links[link]
        landing = slot_at[((da - ma) % side, (db - mb) % side)]
        return pltpu.make_async_remote_copy(
            src_ref=source,
            dst_ref=rows.at[landing, pl.ds(part * piece_rows, piece_rows), :],
            send_sem=send_sem.at[send_plan[(group, part, link)]],
            recv_sem=arrive_sem.at[landing * pieces + part],
            device_id=(req, device_at(ma, mb, False)), device_id_type=mesh_ids)

    def arrived(slot, part):
        here = rows.at[slot, pl.ds(part * piece_rows, piece_rows), :]
        return pltpu.make_async_copy(here, here, arrive_sem.at[slot * pieces + part])

    def tag_copy(group, link):
        da, db = group
        if link == "partner":
            landing = slot_at[(db, da)] * 2 + 1
            target = device_at(0, 0, True)
        else:
            ma, mb = links[link]
            landing = slot_at[((da - ma) % side, (db - mb) % side)] * 2
            target = device_at(ma, mb, False)
        return pltpu.make_async_remote_copy(
            src_ref=tags.at[slot_at[group] * 2], dst_ref=tags.at[landing],
            send_sem=tag_send.at[tag_plan[(group, link)]], recv_sem=tag_recv.at[landing],
            device_id=(req, target), device_id_type=mesh_ids)

    def tag_here(landing):
        return pltpu.make_async_copy(tags.at[landing], tags.at[landing], tag_recv.at[landing])

    def send_onward(da, db, part):
        for link in onward(da, db, part):
            piece_copy((da, db), part, link).start()
        piece_copy((da, db), part, "partner").start()
        for link in ["partner"] + list(range(4)):
            if part == 0 and (((da, db), link) in tag_plan):
                tag_copy((da, db), link).start()

    for part in range(pieces):
        send_onward(0, 0, part)

    weight_copy.wait()

    def stat_copy(group, other):
        owner = device_at(group[0], group[1], other)
        index = slot_at[group] * 2 + other
        return pltpu.make_async_remote_copy(
            src_ref=own_stats.at[slot_at[group], other], dst_ref=stats_in.at[me],
            send_sem=stat_send.at[index], recv_sem=stat_recv,
            device_id=(req, owner), device_id_type=mesh_ids)

    first_column = me * columns

    def one_group(step, carry):
        for index in range(len(group_order)):
            if arrivals[index]:
                @pl.when(step == index)
                def _():
                    for da, db, part in arrivals[index]:
                        arrived(slot_at[(da, db)], part).wait()
                        if part == 0:
                            tag_here(slot_at[(da, db)] * 2).wait()
                        send_onward(da, db, part)

        for part in range(pieces):
            there = rows.at[step, pl.ds(cap + part * piece_rows, piece_rows), :]
            pltpu.make_async_copy(there, there, partner_sem.at[step * pieces + part]).wait()
        tag_here(step * 2 + 1).wait()

        @pl.when(step == len(group_order) - 1)
        def _():
            for ahead in range(1, side):
                pl.semaphore_signal(token, inc=1, device_id=(lax.rem(req + ahead, side), me), device_id_type=mesh_ids)

        logits = lax.dot_general(weight_t[...], rows[step], (((1,), (1,)), ((), ())), preferred_element_type=f32)
        for other in range(2):
            part_logits = logits[:, other * cap:(other + 1) * cap]
            tag = tags[step * 2 + other] - first_column
            peak = jnp.max(part_logits, axis=0, keepdims=True)
            shifted = part_logits - peak
            exponent = jnp.exp(shifted)
            total = jnp.sum(exponent, axis=0, keepdims=True)
            spread = jnp.sum(exponent * shifted, axis=0, keepdims=True)
            column = lax.broadcasted_iota(jnp.int32, part_logits.shape, 0)
            picked = jnp.sum(jnp.where(column == tag, part_logits, 0.0), axis=0, keepdims=True)
            own_stats[step, other] = jnp.concatenate([peak, total, spread, picked] * 2, axis=0)

        for index, group in enumerate(group_order):
            @pl.when(step == index)
            def _():
                for other in range(2):
                    if index == 0 and other == 0:
                        stats_in[me] = own_stats[0, 0]
                    else:
                        stat_copy(group, other).start()
        return carry

    lax.fori_loop(0, len(group_order), one_group, 0)

    pltpu.make_async_copy(stats_in.at[pl.ds(0, members - 1)], stats_in.at[pl.ds(0, members - 1)], stat_recv).wait()

    peak = stats_in[0]
    for index in range(1, members):
        peak = jnp.maximum(peak, stats_in[index])
    peak = peak[0:1]
    row_total = jnp.zeros((1, cap), f32)
    spread = jnp.zeros((1, cap), f32)
    picked = jnp.zeros((1, cap), f32)
    for index in range(members):
        tile = stats_in[index]
        below = tile[0:1] - peak
        factor = jnp.exp(below)
        row_total = row_total + tile[1:2] * factor
        spread = spread + factor * (tile[2:3] + below * tile[1:2])
        picked = picked + tile[3:4]
    log_total = jnp.log(row_total)
    logprob = jnp.broadcast_to(picked - peak - log_total, (seq_count, cap))
    entropy = jnp.broadcast_to(log_total - spread / row_total, (seq_count, cap))

    request = lax.broadcasted_iota(jnp.int32, (seq_count, cap), 0)
    lane = lax.broadcasted_iota(jnp.int32, (seq_count, cap), 1)
    offset = jnp.zeros((seq_count, cap), jnp.int32)
    length = jnp.zeros((seq_count, cap), jnp.int32)
    for seq in range(seq_count):
        offset = jnp.where(request == seq, offsets[seq], offset)
        length = jnp.where(request == seq, lens[seq], length)
    bit = 1
    while bit < cap:
        moved = (offset & bit) != 0
        logprob = jnp.where(moved, pltpu.roll(logprob, cap - bit, 1), logprob)
        entropy = jnp.where(moved, pltpu.roll(entropy, cap - bit, 1), entropy)
        bit *= 2
    logprob = jnp.where(lane < length, logprob, 0.0)
    entropy = jnp.where(lane < length, entropy, 0.0)
    both = logprob + pltpu.roll(entropy, seq_len, 1)
    half = seq_count // 2
    fin[req * members + me] = both[:half] + pltpu.roll(both[half:], cap // 2, 1)

    pl.semaphore_wait(token, side - 1)
    mine = req * members + me

    def fin_copy(step):
        other = lax.rem(mine + step, members * side)
        return pltpu.make_async_remote_copy(
            src_ref=fin.at[mine], dst_ref=fin.at[mine], send_sem=fin_send, recv_sem=fin_recv,
            device_id=(other // members, lax.rem(other, members)), device_id_type=mesh_ids)

    def send_fin(step, carry):
        fin_copy(step).start()
        return carry

    lax.fori_loop(1, members * side, send_fin, 0)
    others = fin.at[pl.ds(0, members * side - 1)]
    pltpu.make_async_copy(others, others, fin_recv).wait()

    for seq in range(seq_count):
        wanted = slots[seq]
        owner = lax.div(wanted, seq_count)
        inside = lax.rem(wanted, seq_count)
        tile = fin[owner]
        turned = pltpu.roll(tile, cap // 2, 1)
        tile = jnp.where(inside >= half, turned, tile)
        level = lax.rem(inside, half)
        row = lax.broadcasted_iota(jnp.int32, (half, cap), 0)
        gathered[pl.ds(seq, 1), :] = jnp.sum(jnp.where(row == level, tile, 0.0), axis=0, keepdims=True)
    out[0] = gathered[:, 0:seq_len]
    out[1] = gathered[:, seq_len:2 * seq_len]

    def drain(index, carry):
        here = rows.at[0, pl.ds(0, piece_rows), :]
        pltpu.make_async_copy(here, here, send_sem.at[index]).wait()
        return carry

    lax.fori_loop(0, send_count, drain, 0)
    def drain_tags(index, carry):
        pltpu.make_async_copy(tags.at[0], tags.at[0], tag_send.at[index]).wait()
        return carry

    lax.fori_loop(0, len(tag_plan), drain_tags, 0)

    def drain_stats(index, carry):
        pltpu.make_async_copy(stats_in.at[0], stats_in.at[0], stat_send.at[index]).wait()
        return carry

    lax.fori_loop(1, 2 * len(group_order), drain_stats, 0)
    pltpu.make_async_copy(others, others, fin_send).wait()


def local(hidden_states, norm_gain, head_weight, targets, lengths, slot_of):
    held, depth = hidden_states.shape
    seq_count = lengths.shape[0]
    seq_len = held // seq_count
    columns = head_weight.shape[1]
    groups = side * side
    members = 2 * groups
    vmem = pl.BlockSpec(memory_space=pltpu.VMEM)
    smem = pl.BlockSpec(memory_space=pltpu.SMEM)
    dma = pltpu.SemaphoreType.DMA
    out = jax.ShapeDtypeStruct((2, seq_count, seq_len), f32)
    both = pl.pallas_call(
        kernel,
        out_shape=out,
        in_specs=[smem, smem, vmem, vmem, vmem, pl.BlockSpec(memory_space=pl.ANY)],
        out_specs=vmem,
        scratch_shapes=[
            pltpu.VMEM((columns, depth), jnp.bfloat16),
            pltpu.VMEM((groups, 2 * cap, depth), jnp.bfloat16),
            pltpu.VMEM((members, 1, cap), jnp.int32),
            pltpu.VMEM((groups, 2, 8, cap), f32),
            pltpu.VMEM((members, 8, cap), f32),
            pltpu.VMEM((members * side, seq_count // 2, cap), f32),
            pltpu.VMEM((seq_count, cap), f32),
            dma,
            dma((send_count,)),
            dma((groups * pieces,)),
            dma((groups * pieces,)),
            dma((len(tag_plan),)),
            dma((members,)),
            dma((members,)),
            dma,
            pltpu.SemaphoreType.REGULAR,
            dma, dma,
        ],
        compiler_params=pltpu.CompilerParams(collective_id=0, has_side_effects=True, vmem_limit_bytes=60 << 20),
        name="head_stats",
    )(lengths, slot_of, hidden_states, norm_gain.reshape(1, depth), targets.reshape(1, held), head_weight.T)
    return (both[0], both[1])


def solution(mesh):
    rows = jax.sharding.PartitionSpec(("req", "vocab"), None)
    flat = jax.sharding.PartitionSpec(("req", "vocab"))
    in_specs = (rows, jax.sharding.PartitionSpec(), jax.sharding.PartitionSpec(None, "vocab"), flat, flat, flat)
    return jax.shard_map(local, mesh=mesh, in_specs=in_specs, out_specs=(rows, rows), check_vma=False)
```

```python
import jax
import jax.numpy as jnp
from jax import lax
from jax.experimental import pallas as pl
from jax.experimental.pallas import tpu as pltpu

eps_norm = 1e-05
side = 4
cap = 128
pieces = 4
piece_rows = cap // pieces
group_count = 2 * side
mesh_ids = pl.DeviceIdType.MESH
f32 = jnp.float32

sub_rows = (32, 32, 16, 32, 64, 32)
part_subs = ((0, 1, 2, 3), (4, 5))
rest_part = 1
steps = [
    ([], 0, 0),
    ([('W', 0, 0), ('R', 1, 0, 0), ('R', 0, 3, 0), ('R', 0, 1, 0), ('W', 0, 1), ('R', 0, 3, 2), ('R', 0, 1, 2), ('R', 1, 0, 2), ('W', 0, 2), ('W', 3, 0), ('W', 1, 0), ('R', 1, 0, 1), ('R', 0, 3, 1), ('R', 0, 1, 1), ('W', 0, 3), ('W', 3, 1), ('W', 1, 1), ('R', 0, 3, 3), ('R', 0, 1, 3), ('R', 1, 0, 3), ('W', 3, 2), ('W', 1, 2)], 0, 1),
    ([], 0, 3),
    ([('R', 1, 3, 0), ('R', 1, 1, 0), ('R', 1, 3, 2), ('W', 2, 0), ('W', 1, 3), ('W', 0, 4)], 0, 4),
    ([('R', 0, 2, 0), ('R', 1, 1, 2), ('R', 1, 1, 1), ('W', 3, 3), ('W', 2, 1), ('W', 0, 5), ('W', 2, 2), ('R', 0, 2, 2), ('R', 0, 2, 1), ('R', 1, 3, 3), ('W', 2, 3)], 1, 0),
    ([], 1, 1),
    ([], 1, 3),
    ([], 1, 4),
    ([('R', 1, 3, 1), ('R', 1, 1, 3), ('R', 0, 2, 3)], 0, 2),
    ([('W', 3, 4)], 0, 5),
    ([('R', 1, 2, 0), ('R', 1, 2, 1), ('R', 1, 2, 2), ('W', 1, 4)], 0, 7),
    ([('W', 3, 5), ('R', 1, 2, 3)], 1, 2),
    ([('W', 1, 5)], 1, 5),
    ([], 0, 6),
    ([], 1, 7),
    ([], 1, 6),
    ([('W', 2, 4), ('W', 2, 5), ('D', 0)], 2, 6),
    ([], 2, 2),
    ([], 2, 5),
    ([], 2, 7),
    ([], 2, 1),
    ([], 2, 3),
    ([], 2, 4),
    ([], 2, 0),
]
sub_start = [sum(sub_rows[:index]) for index in range(len(sub_rows))]
quarter = sum(sub_rows)
part_of_sub = {sub: part for part, subs in enumerate(part_subs) for sub in subs}
part_block = [sum(sub_rows[sub] for sub in subs) for subs in part_subs]


def row_links(p, dy, q):
    taken = []
    x_first = q < 2
    upward = q % 2 == 0
    if x_first:
        if (p, dy) == (0, 0):
            taken.append("x")
        if dy == 0:
            taken += ["up", "down"]
    else:
        if (p, dy) == (0, 0):
            taken += ["up", "down"]
        if p == 0:
            taken.append("x")
    if x_first or p == 0:
        if dy == 3 and upward:
            taken.append("up")
        if dy == 1 and not upward:
            taken.append("down")
    return taken


def row_landing(p, dy, link):
    if link == "x":
        return (1 - p, dy)
    if link == "partner":
        return (p, dy)
    return (p, (dy + (3 if link == "up" else 1)) % side)


def weight_links(d, sub):
    if d == 0:
        return ["up", "down"]
    if d == 3 and sub % 2 == 0:
        return ["up"]
    if d == 1 and sub % 2 == 1:
        return ["down"]
    return []


def weight_landing(d, link):
    return (d + (3 if link == "up" else 1)) % side


all_groups = [(p, dy) for p in range(2) for dy in range(side)]
row_plan = {}
tag_plan = {}
tag_first = {}
for plan_group in all_groups:
    for plan_link in ["partner", "x", "up", "down"]:
        for plan_piece in range(pieces):
            if plan_link == "partner" or plan_link in row_links(*plan_group, plan_piece):
                row_plan[(plan_group, plan_piece, plan_link)] = len(row_plan)
                landing_group = row_landing(*plan_group, plan_link)
                if plan_piece == 0:
                    tag_plan[(plan_group, plan_link)] = len(tag_plan)
weight_arrivals = [(d, sub) for d in range(side) for sub in range(len(sub_rows))]
weight_slot = {arrival: index for index, arrival in enumerate(weight_arrivals)}
rest_slot = len(weight_arrivals)
weight_plan = {}
for plan_arrival in weight_arrivals:
    for plan_link in weight_links(*plan_arrival):
        weight_plan[(plan_arrival, plan_link)] = len(weight_plan)
entry_plan = {sub: len(weight_plan) + sub for sub in range(len(sub_rows))}
rest_plan = len(weight_plan) + len(sub_rows)
weight_sends = rest_plan + 1
last_part = len(part_subs)
last_own_step = max(index for index, step_entry in enumerate(steps) if step_entry[1] == 0)


def kernel(lens, slots, hidden, gain, targets, weight_hbm, out, *scratch):
    weight_t, rows, tags, running, stats_in, fin, gathered = scratch[:7]
    pair_parts = scratch[7:7 + len(part_subs)]
    (weight_sem, row_send, row_recv, partner_recv, weight_send, weight_recv, tag_send, tag_recv,
     stat_send, stat_recv, token_x, token_z, fin_send, fin_recv) = scratch[7 + len(part_subs):]
    req = lax.axis_index("req")
    me = lax.axis_index("vocab")
    core = lax.rem(me, 2)
    chip_x = lax.rem(me // 2, side)
    chip_y = me // (2 * side)
    members = 2 * side * side
    columns, depth = weight_t.shape
    side_x = lax.rem(chip_x, 2)
    pair_x = side - 1 - chip_x

    def vocab_id(x, y, the_core):
        return (y * side + x) * 2 + the_core

    def group_owner(group, other):
        p, dy = group
        x = chip_x + p * (1 - 2 * side_x)
        return vocab_id(x, lax.rem(chip_y + dy, side), (1 - core) if other else core)

    def row_target(link):
        if link == "partner":
            return (req, vocab_id(chip_x, chip_y, 1 - core))
        if link == "x":
            return (req, group_owner((1, 0), False))
        return (req, group_owner((0, 1 if link == "up" else 3), False))

    def z_target(ahead):
        return (lax.rem(req + ahead, side), me)

    pair_target = (req, vocab_id(pair_x, chip_y, core))

    barrier = pltpu.get_barrier_semaphore()
    neighbours = [row_target(link) for link in ("partner", "x", "up", "down")] + [pair_target, z_target(1), z_target(3)]
    for neighbour in neighbours:
        pl.semaphore_signal(barrier, inc=1, device_id=neighbour, device_id_type=mesh_ids)

    weight_copy = pltpu.make_async_copy(weight_hbm, weight_t, weight_sem)
    weight_copy.start()

    seq_count = lens.shape[0]
    held = hidden.shape[0]
    seq_len = held // seq_count
    offsets = []
    total_length = jnp.int32(0)
    for seq in range(seq_count):
        offsets.append(total_length)
        total_length = total_length + lens[seq]

    def compact_place(slot_index):
        place = jnp.full(slot_index.shape, -1, jnp.int32)
        for seq in range(seq_count):
            ahead = slot_index - seq * seq_len
            place = jnp.where((ahead >= 0) & (ahead < lens[seq]), ahead + offsets[seq], place)
        return place

    place_row = compact_place(lax.broadcasted_iota(jnp.int32, (8, held), 1))[:1]
    pick = (lax.broadcasted_iota(jnp.int32, (cap, held), 0) == place_row).astype(f32).astype(jnp.bfloat16)
    live = jnp.dot(pick, hidden[...], preferred_element_type=f32)
    inverse_rms = lax.rsqrt(jnp.mean(live * live, axis=1, keepdims=True) + eps_norm)
    rows[0, 0:cap, :] = (live * inverse_rms * gain[...]).astype(jnp.bfloat16)

    place_col = compact_place(lax.broadcasted_iota(jnp.int32, (held, cap), 0))
    pick_t = (lax.broadcasted_iota(jnp.int32, (held, cap), 1) == place_col).astype(f32).astype(jnp.bfloat16)
    wide = targets[...]
    high = wide // 256
    digits = jnp.concatenate([high, wide - high * 256] + [jnp.zeros_like(wide)] * 14, axis=0)
    digits = digits.astype(f32).astype(jnp.bfloat16)
    tag_pair = jnp.dot(digits, pick_t, preferred_element_type=f32)
    tags[0] = (tag_pair[0:1] * 256.0 + tag_pair[1:2]).astype(jnp.int32)

    pl.semaphore_wait(barrier, len(neighbours))

    def part_rows(d, sub):
        part = part_of_sub[sub]
        start = d * part_block[part] + sub_start[sub] - sub_start[part_subs[part][0]]
        return pair_parts[part].at[pl.ds(start, sub_rows[sub]), :]

    def rest_rows():
        return pair_parts[rest_part].at[pl.ds(side * part_block[rest_part], columns - side * quarter), :]

    def entry_copy(sub):
        start = pl.multiple_of(req * quarter + sub_start[sub], 16)
        return pltpu.make_async_remote_copy(
            src_ref=weight_hbm.at[pl.ds(start, sub_rows[sub]), :], dst_ref=part_rows(0, sub),
            send_sem=weight_send.at[entry_plan[sub]], recv_sem=weight_recv.at[weight_slot[(0, sub)]],
            device_id=pair_target, device_id_type=mesh_ids)

    def rest_copy():
        return pltpu.make_async_remote_copy(
            src_ref=weight_hbm.at[pl.ds(side * quarter, columns - side * quarter), :], dst_ref=rest_rows(),
            send_sem=weight_send.at[rest_plan], recv_sem=weight_recv.at[rest_slot],
            device_id=pair_target, device_id_type=mesh_ids)

    def weight_relay(d, sub, link):
        landing = weight_landing(d, link)
        return pltpu.make_async_remote_copy(
            src_ref=part_rows(d, sub), dst_ref=part_rows(landing, sub),
            send_sem=weight_send.at[weight_plan[((d, sub), link)]], recv_sem=weight_recv.at[weight_slot[(landing, sub)]],
            device_id=z_target(1 if link == "up" else 3), device_id_type=mesh_ids)

    def row_index(group):
        return group[0] * side + group[1]

    def piece_copy(group, piece, link):
        landing = row_index(row_landing(*group, link))
        start = piece * piece_rows
        there = start + (cap if link == "partner" else 0)
        recv = (partner_recv if link == "partner" else row_recv).at[landing * pieces + piece]
        return pltpu.make_async_remote_copy(
            src_ref=rows.at[row_index(group), pl.ds(start, piece_rows), :],
            dst_ref=rows.at[landing, pl.ds(there, piece_rows), :],
            send_sem=row_send.at[row_plan[(group, piece, link)]], recv_sem=recv,
            device_id=row_target(link), device_id_type=mesh_ids)

    def tag_copy(group, link):
        landing = row_index(row_landing(*group, link)) * 2 + (1 if link == "partner" else 0)
        return pltpu.make_async_remote_copy(
            src_ref=tags.at[row_index(group) * 2], dst_ref=tags.at[landing],
            send_sem=tag_send.at[tag_plan[(group, link)]], recv_sem=tag_recv.at[landing],
            device_id=row_target(link), device_id_type=mesh_ids)

    def tag_here(landing):
        return pltpu.make_async_copy(tags.at[landing], tags.at[landing], tag_recv.at[landing])

    def send_onward(p, dy, piece):
        taken = row_links(p, dy, piece) + ["partner"]
        for link in taken:
            piece_copy((p, dy), piece, link).start()
        if piece == 0:
            for link in taken:
                tag_copy((p, dy), link).start()

    entry_copy(0).start()
    for piece in (0, 2, 1, 3):
        send_onward(0, 0, piece)
    for sub in range(1, len(sub_rows)):
        entry_copy(sub).start()
    rest_copy().start()

    weight_copy.wait()

    def arrival(event):
        if event[0] == "D":
            pltpu.make_async_copy(rest_rows(), rest_rows(), weight_recv.at[rest_slot]).wait()
        elif event[0] == "W":
            here = part_rows(event[1], event[2])
            pltpu.make_async_copy(here, here, weight_recv.at[weight_slot[event[1:]]]).wait()
            for link in weight_links(*event[1:]):
                weight_relay(event[1], event[2], link).start()
        else:
            group, piece = event[1:3], event[3]
            here = rows.at[row_index(group), pl.ds(piece * piece_rows, piece_rows), :]
            pltpu.make_async_copy(here, here, row_recv.at[row_index(group) * pieces + piece]).wait()
            if piece == 0:
                tag_here(row_index(group) * 2).wait()
            send_onward(*group, piece)

    my_place = (chip_y * 2 + side_x) * 2 + core

    def stat_copy(group, other):
        return pltpu.make_async_remote_copy(
            src_ref=running.at[row_index(group), other], dst_ref=stats_in.at[my_place],
            send_sem=stat_send.at[row_index(group) * 2 + other], recv_sem=stat_recv,
            device_id=(req, group_owner(group, other)), device_id_type=mesh_ids)

    own_first = me * columns
    pair_first = vocab_id(pair_x, chip_y, core) * columns
    own_blocks = [(0, columns, own_first)]

    def part_blocks(part):
        blocks = []
        for d in range(side):
            first = pair_first + lax.rem(req + d, side) * quarter + sub_start[part_subs[part][0]]
            blocks.append((d * part_block[part], part_block[part], first))
        if part == rest_part:
            blocks.append((side * part_block[part], columns - side * quarter, pair_first + side * quarter))
        return blocks

    def tile(group, weight_ref, blocks, fresh):
        logits = lax.dot_general(weight_ref[...], rows[group], (((1,), (1,)), ((), ())), preferred_element_type=f32)
        for other in range(2):
            piece = logits[:, other * cap:(other + 1) * cap]
            tag = tags[group * 2 + other]
            peak = jnp.max(piece, axis=0, keepdims=True)
            shifted = piece - peak
            exponent = jnp.exp(shifted)
            total = jnp.sum(exponent, axis=0, keepdims=True)
            spread = jnp.sum(exponent * shifted, axis=0, keepdims=True)
            picked = jnp.zeros((1, cap), f32)
            for start, size, first in blocks:
                column = lax.broadcasted_iota(jnp.int32, (size, cap), 0)
                block = piece[start:start + size]
                picked = picked + jnp.sum(jnp.where(column == tag - first, block, 0.0), axis=0, keepdims=True)
            if not fresh:
                before = running[group, other]
                joint = jnp.maximum(before[0:1], peak)
                drop_before = before[0:1] - joint
                drop = peak - joint
                factor_before = jnp.exp(drop_before)
                factor = jnp.exp(drop)
                spread = factor_before * (before[2:3] + drop_before * before[1:2]) + factor * (spread + drop * total)
                total = factor_before * before[1:2] + factor * total
                picked = picked + before[3:4]
                peak = joint
            running[group, other] = jnp.concatenate([peak, total, spread, picked] * 2, axis=0)

    def one_step(step, carry):
        for index, (events, kind, group) in enumerate(steps):
            if events:
                @pl.when(step == index)
                def _():
                    for event in events:
                        arrival(event)

        code = jnp.int32(0)
        for index, (events, kind, group) in enumerate(steps):
            code = jnp.where(step == index, kind * group_count + group, code)
        kind_now = code // group_count
        group_now = lax.rem(code, group_count)

        @pl.when(kind_now == 0)
        def _():
            for piece in range(pieces):
                there = rows.at[group_now, pl.ds(cap + piece * piece_rows, piece_rows), :]
                pltpu.make_async_copy(there, there, partner_recv.at[group_now * pieces + piece]).wait()
            landing = group_now * 2 + 1
            pltpu.make_async_copy(tags.at[landing], tags.at[landing], tag_recv.at[landing]).wait()
            tile(group_now, weight_t, own_blocks, True)

        for part in range(len(part_subs)):
            @pl.when(kind_now == part + 1)
            def _():
                tile(group_now, pair_parts[part], part_blocks(part), False)

        for index, (events, kind, group) in enumerate(steps):
            if kind == last_part:
                @pl.when(step == index)
                def _():
                    for other in range(2):
                        if group == 0 and other == 0:
                            stats_in[my_place] = running[0, 0]
                        else:
                            stat_copy(all_groups[group], other).start()

        @pl.when(step == last_own_step)
        def _():
            pl.semaphore_signal(token_x, inc=1, device_id=pair_target, device_id_type=mesh_ids)

        @pl.when(step == len(steps) - 3)
        def _():
            pl.semaphore_wait(token_x, 1)
            for ahead in range(1, side):
                pl.semaphore_signal(token_z, inc=1, device_id=z_target(ahead), device_id_type=mesh_ids)
        return carry

    lax.fori_loop(0, len(steps), one_step, 0)

    sources = 2 * group_count
    pltpu.make_async_copy(stats_in.at[pl.ds(0, sources - 1)], stats_in.at[pl.ds(0, sources - 1)], stat_recv).wait()

    peak = stats_in[0]
    for index in range(1, sources):
        peak = jnp.maximum(peak, stats_in[index])
    peak = peak[0:1]
    row_total = jnp.zeros((1, cap), f32)
    spread = jnp.zeros((1, cap), f32)
    picked = jnp.zeros((1, cap), f32)
    for index in range(sources):
        stat = stats_in[index]
        below = stat[0:1] - peak
        factor = jnp.exp(below)
        row_total = row_total + stat[1:2] * factor
        spread = spread + factor * (stat[2:3] + below * stat[1:2])
        picked = picked + stat[3:4]
    log_total = jnp.log(row_total)
    logprob = jnp.broadcast_to(picked - peak - log_total, (seq_count, cap))
    entropy = jnp.broadcast_to(log_total - spread / row_total, (seq_count, cap))

    request = lax.broadcasted_iota(jnp.int32, (seq_count, cap), 0)
    lane = lax.broadcasted_iota(jnp.int32, (seq_count, cap), 1)
    offset = jnp.zeros((seq_count, cap), jnp.int32)
    length = jnp.zeros((seq_count, cap), jnp.int32)
    for seq in range(seq_count):
        offset = jnp.where(request == seq, offsets[seq], offset)
        length = jnp.where(request == seq, lens[seq], length)
    bit = 1
    while bit < cap:
        moved = (offset & bit) != 0
        logprob = jnp.where(moved, pltpu.roll(logprob, cap - bit, 1), logprob)
        entropy = jnp.where(moved, pltpu.roll(entropy, cap - bit, 1), entropy)
        bit *= 2
    logprob = jnp.where(lane < length, logprob, 0.0)
    entropy = jnp.where(lane < length, entropy, 0.0)
    both = logprob + pltpu.roll(entropy, seq_len, 1)
    half = seq_count // 2
    mine = req * members + me
    fin[mine] = both[:half] + pltpu.roll(both[half:], cap // 2, 1)

    pl.semaphore_wait(token_z, side - 1)

    def fin_copy(step):
        other = lax.rem(mine + step, members * side)
        return pltpu.make_async_remote_copy(
            src_ref=fin.at[mine], dst_ref=fin.at[mine], send_sem=fin_send, recv_sem=fin_recv,
            device_id=(other // members, lax.rem(other, members)), device_id_type=mesh_ids)

    def send_fin(step, carry):
        fin_copy(step).start()
        return carry

    lax.fori_loop(1, members * side, send_fin, 0)
    others = fin.at[pl.ds(0, members * side - 1)]
    pltpu.make_async_copy(others, others, fin_recv).wait()

    for seq in range(seq_count):
        wanted = slots[seq]
        owner = lax.div(wanted, seq_count)
        inside = lax.rem(wanted, seq_count)
        found = fin[owner]
        turned = pltpu.roll(found, cap // 2, 1)
        found = jnp.where(inside >= half, turned, found)
        level = lax.rem(inside, half)
        row = lax.broadcasted_iota(jnp.int32, (half, cap), 0)
        gathered[pl.ds(seq, 1), :] = jnp.sum(jnp.where(row == level, found, 0.0), axis=0, keepdims=True)
    out[0] = gathered[:, 0:seq_len]
    out[1] = gathered[:, seq_len:2 * seq_len]

    def drain(index, carry):
        here = rows.at[0, pl.ds(0, piece_rows), :]
        pltpu.make_async_copy(here, here, row_send.at[index]).wait()
        return carry

    lax.fori_loop(0, len(row_plan), drain, 0)
    for (d, sub), link in weight_plan:
        weight_relay(d, sub, link).wait_send()
    for sub in range(len(sub_rows)):
        entry_copy(sub).wait_send()
    rest_copy().wait_send()

    def drain_tags(index, carry):
        pltpu.make_async_copy(tags.at[0], tags.at[0], tag_send.at[index]).wait()
        return carry

    lax.fori_loop(0, len(tag_plan), drain_tags, 0)

    def drain_stats(index, carry):
        pltpu.make_async_copy(stats_in.at[0], stats_in.at[0], stat_send.at[index]).wait()
        return carry

    lax.fori_loop(1, sources, drain_stats, 0)
    pltpu.make_async_copy(others, others, fin_send).wait()


def local(hidden_states, norm_gain, head_weight, targets, lengths, slot_of):
    held, depth = hidden_states.shape
    seq_count = lengths.shape[0]
    seq_len = held // seq_count
    columns = head_weight.shape[1]
    members = 2 * side * side
    vmem = pl.BlockSpec(memory_space=pltpu.VMEM)
    smem = pl.BlockSpec(memory_space=pltpu.SMEM)
    dma = pltpu.SemaphoreType.DMA
    regular = pltpu.SemaphoreType.REGULAR
    part_sizes = [side * block + (columns - side * quarter if part == rest_part else 0)
                  for part, block in enumerate(part_block)]
    out = jax.ShapeDtypeStruct((2, seq_count, seq_len), f32)
    both = pl.pallas_call(
        kernel,
        out_shape=out,
        in_specs=[smem, smem, vmem, vmem, vmem, pl.BlockSpec(memory_space=pl.ANY)],
        out_specs=vmem,
        scratch_shapes=[
            pltpu.VMEM((columns, depth), jnp.bfloat16),
            pltpu.VMEM((group_count, 2 * cap, depth), jnp.bfloat16),
            pltpu.VMEM((2 * group_count, 1, cap), jnp.int32),
            pltpu.VMEM((group_count, 2, 8, cap), f32),
            pltpu.VMEM((2 * group_count, 8, cap), f32),
            pltpu.VMEM((members * side, seq_count // 2, cap), f32),
            pltpu.VMEM((seq_count, cap), f32),
        ] + [pltpu.VMEM((size, depth), jnp.bfloat16) for size in part_sizes] + [
            dma,
            dma((len(row_plan),)),
            dma((group_count * pieces,)),
            dma((group_count * pieces,)),
            dma((weight_sends,)),
            dma((rest_slot + 1,)),
            dma((len(tag_plan),)),
            dma((2 * group_count,)),
            dma((2 * group_count,)),
            dma,
            regular,
            regular,
            dma,
            dma,
        ],
        compiler_params=pltpu.CompilerParams(collective_id=0, has_side_effects=True, vmem_limit_bytes=60 << 20),
        name="head_stats",
    )(lengths, slot_of, hidden_states, norm_gain.reshape(1, depth), targets.reshape(1, held), head_weight.T)
    return (both[0], both[1])


def solution(mesh):
    rows = jax.sharding.PartitionSpec(("req", "vocab"), None)
    flat = jax.sharding.PartitionSpec(("req", "vocab"))
    in_specs = (rows, jax.sharding.PartitionSpec(), jax.sharding.PartitionSpec(None, "vocab"), flat, flat, flat)
    return jax.shard_map(local, mesh=mesh, in_specs=in_specs, out_specs=(rows, rows), check_vma=False)
```

```python
import jax
import jax.numpy as jnp
from jax import lax
from jax.experimental import pallas as pl
from jax.experimental.pallas import tpu as pltpu

eps_norm = 1e-05
side = 4
cap = 128
pieces = 4
piece_rows = cap // pieces
group_count = 2 * side
mesh_ids = pl.DeviceIdType.MESH
f32 = jnp.float32

sub_rows = (32, 32, 32, 32, 48, 32)
rest_rows = (80, 88)
entries = [("W", 0, 0), ("W", 0, 1), ("W", 0, 2), ("W", 0, 3), ("W", 0, 4), ("D", 0), ("W", 0, 5), ("D", 1)]
parts = [[("W", 0, 0), ("W", 0, 1), ("W", 3, 0), ("W", 1, 0), ("W", 0, 2), ("W", 3, 1), ("W", 1, 1), ("W", 0, 3), ("W", 2, 0), ("W", 1, 2), ("W", 0, 4), ("W", 3, 2), ("W", 2, 1), ("W", 3, 3), ("W", 1, 3)], [("D", 0)], [("W", 3, 4), ("W", 1, 4), ("W", 0, 5), ("W", 2, 2), ("W", 2, 3), ("W", 1, 5), ("W", 2, 4), ("W", 3, 5), ("D", 1), ("W", 2, 5)]]
steps = [
    ([], 0, 0),
    ([("W", 0, 0), ("R", 1, 0, 0), ("R", 0, 3, 0), ("R", 0, 1, 0), ("W", 0, 1), ("R", 0, 3, 2), ("R", 0, 1, 2), ("R", 1, 0, 2), ("W", 3, 0), ("W", 1, 0), ("W", 0, 2), ("R", 1, 0, 1), ("R", 0, 3, 1), ("R", 0, 1, 1), ("W", 3, 1), ("W", 1, 1), ("W", 0, 3), ("R", 0, 3, 3), ("R", 0, 1, 3), ("R", 1, 0, 3)], 0, 1),
    ([("W", 2, 0), ("W", 1, 2), ("R", 1, 3, 0), ("R", 1, 1, 0), ("R", 1, 3, 2)], 0, 3),
    ([("W", 0, 4), ("W", 3, 2), ("W", 2, 1)], 0, 4),
    ([("R", 0, 2, 0), ("R", 1, 1, 2), ("R", 1, 1, 1), ("W", 3, 3), ("W", 1, 3)], 1, 0),
    ([], 1, 1),
    ([("R", 0, 2, 2), ("R", 0, 2, 1), ("R", 1, 3, 3)], 1, 3),
    ([], 1, 4),
    ([("D", 0), ("R", 1, 3, 1), ("R", 1, 1, 3), ("R", 0, 2, 3)], 2, 0),
    ([("W", 3, 4), ("W", 1, 4)], 2, 1),
    ([], 2, 3),
    ([], 2, 4),
    ([], 0, 2),
    ([("W", 0, 5), ("R", 1, 2, 0), ("R", 1, 2, 1), ("R", 1, 2, 2)], 0, 5),
    ([("W", 2, 2), ("W", 2, 3)], 0, 7),
    ([("R", 1, 2, 3)], 1, 2),
    ([], 1, 5),
    ([("W", 1, 5), ("W", 2, 4)], 0, 6),
    ([], 1, 7),
    ([("W", 3, 5)], 1, 6),
    ([("D", 1)], 2, 2),
    ([], 2, 5),
    ([("W", 2, 5)], 2, 7),
    ([], 2, 6),
    ([], 3, 6),
    ([], 3, 2),
    ([], 3, 5),
    ([], 3, 7),
    ([], 3, 1),
    ([], 3, 3),
    ([], 3, 4),
    ([], 3, 0),
]
sub_start = [sum(sub_rows[:index]) for index in range(len(sub_rows))]
quarter = sum(sub_rows)
part_place = {}
part_sizes = []
for part_index, part_list in enumerate(parts):
    filled = 0
    for part_piece in part_list:
        part_place[part_piece] = (part_index, filled)
        filled += sub_rows[part_piece[2]] if part_piece[0] == "W" else rest_rows[part_piece[1]]
    part_sizes.append(filled)
rest_start = [side * quarter + sum(rest_rows[:index]) for index in range(len(rest_rows))]


def row_links(p, dy, q):
    taken = []
    x_first = q < 2
    upward = q % 2 == 0
    if x_first:
        if (p, dy) == (0, 0):
            taken.append("x")
        if dy == 0:
            taken += ["up", "down"]
    else:
        if (p, dy) == (0, 0):
            taken += ["up", "down"]
        if p == 0:
            taken.append("x")
    if x_first or p == 0:
        if dy == 3 and upward:
            taken.append("up")
        if dy == 1 and not upward:
            taken.append("down")
    return taken


def row_landing(p, dy, link):
    if link == "x":
        return (1 - p, dy)
    if link == "partner":
        return (p, dy)
    return (p, (dy + (3 if link == "up" else 1)) % side)


def weight_links(d, sub):
    if d == 0:
        return ["up", "down"]
    if d == 3 and sub % 2 == 0:
        return ["up"]
    if d == 1 and sub % 2 == 1:
        return ["down"]
    return []


def weight_landing(d, link):
    return (d + (3 if link == "up" else 1)) % side


all_groups = [(p, dy) for p in range(2) for dy in range(side)]
row_plan = {}
tag_plan = {}
tag_first = {}
for plan_group in all_groups:
    for plan_link in ["partner", "x", "up", "down"]:
        for plan_piece in range(pieces):
            if plan_link == "partner" or plan_link in row_links(*plan_group, plan_piece):
                row_plan[(plan_group, plan_piece, plan_link)] = len(row_plan)
                landing_group = row_landing(*plan_group, plan_link)
                if plan_piece == 0:
                    tag_plan[(plan_group, plan_link)] = len(tag_plan)
weight_arrivals = [(d, sub) for d in range(side) for sub in range(len(sub_rows))]
weight_slot = {arrival: index for index, arrival in enumerate(weight_arrivals)}
rest_slots = [len(weight_arrivals) + index for index in range(len(rest_rows))]
weight_plan = {}
for plan_arrival in weight_arrivals:
    for plan_link in weight_links(*plan_arrival):
        weight_plan[(plan_arrival, plan_link)] = len(weight_plan)
entry_plan = {sub: len(weight_plan) + sub for sub in range(len(sub_rows))}
rest_plan = [len(weight_plan) + len(sub_rows) + index for index in range(len(rest_rows))]
weight_sends = rest_plan[-1] + 1
last_part = len(parts)
last_own_step = max(index for index, step_entry in enumerate(steps) if step_entry[1] == 0)


def kernel(lens, slots, hidden, gain, targets, weight_hbm, out, *scratch):
    weight_t, rows, tags, running, stats_in, fin, gathered = scratch[:7]
    pair_parts = scratch[7:7 + len(parts)]
    (weight_sem, row_send, row_recv, partner_recv, weight_send, weight_recv, tag_send, tag_recv,
     stat_send, stat_recv, token_x, token_z, fin_send, fin_recv) = scratch[7 + len(parts):]
    req = lax.axis_index("req")
    me = lax.axis_index("vocab")
    core = lax.rem(me, 2)
    chip_x = lax.rem(me // 2, side)
    chip_y = me // (2 * side)
    members = 2 * side * side
    columns, depth = weight_t.shape
    side_x = lax.rem(chip_x, 2)
    pair_x = side - 1 - chip_x

    def vocab_id(x, y, the_core):
        return (y * side + x) * 2 + the_core

    def group_owner(group, other):
        p, dy = group
        x = chip_x + p * (1 - 2 * side_x)
        return vocab_id(x, lax.rem(chip_y + dy, side), (1 - core) if other else core)

    def row_target(link):
        if link == "partner":
            return (req, vocab_id(chip_x, chip_y, 1 - core))
        if link == "x":
            return (req, group_owner((1, 0), False))
        return (req, group_owner((0, 1 if link == "up" else 3), False))

    def z_target(ahead):
        return (lax.rem(req + ahead, side), me)

    pair_target = (req, vocab_id(pair_x, chip_y, core))

    barrier = pltpu.get_barrier_semaphore()
    neighbours = [row_target(link) for link in ("partner", "x", "up", "down")] + [pair_target, z_target(1), z_target(3)]
    for neighbour in neighbours:
        pl.semaphore_signal(barrier, inc=1, device_id=neighbour, device_id_type=mesh_ids)

    weight_copy = pltpu.make_async_copy(weight_hbm, weight_t, weight_sem)
    weight_copy.start()

    seq_count = lens.shape[0]
    held = hidden.shape[0]
    seq_len = held // seq_count
    offsets = []
    total_length = jnp.int32(0)
    for seq in range(seq_count):
        offsets.append(total_length)
        total_length = total_length + lens[seq]

    def compact_place(slot_index):
        place = jnp.full(slot_index.shape, -1, jnp.int32)
        for seq in range(seq_count):
            ahead = slot_index - seq * seq_len
            place = jnp.where((ahead >= 0) & (ahead < lens[seq]), ahead + offsets[seq], place)
        return place

    place_row = compact_place(lax.broadcasted_iota(jnp.int32, (8, held), 1))[:1]
    pick = (lax.broadcasted_iota(jnp.int32, (cap, held), 0) == place_row).astype(f32).astype(jnp.bfloat16)
    live = jnp.dot(pick, hidden[...], preferred_element_type=f32)
    inverse_rms = lax.rsqrt(jnp.mean(live * live, axis=1, keepdims=True) + eps_norm)
    rows[0, 0:cap, :] = (live * inverse_rms * gain[...]).astype(jnp.bfloat16)

    place_col = compact_place(lax.broadcasted_iota(jnp.int32, (held, cap), 0))
    pick_t = (lax.broadcasted_iota(jnp.int32, (held, cap), 1) == place_col).astype(f32).astype(jnp.bfloat16)
    wide = targets[...]
    high = wide // 256
    digits = jnp.concatenate([high, wide - high * 256] + [jnp.zeros_like(wide)] * 14, axis=0)
    digits = digits.astype(f32).astype(jnp.bfloat16)
    tag_pair = jnp.dot(digits, pick_t, preferred_element_type=f32)
    tags[0] = (tag_pair[0:1] * 256.0 + tag_pair[1:2]).astype(jnp.int32)

    pl.semaphore_wait(barrier, len(neighbours))

    def part_rows(arrival_name):
        part, start = part_place[arrival_name]
        size = sub_rows[arrival_name[2]] if arrival_name[0] == "W" else rest_rows[arrival_name[1]]
        return pair_parts[part].at[pl.ds(start, size), :]

    def entry_copy(name):
        if name[0] == "W":
            sub = name[2]
            start, size = pl.multiple_of(req * quarter + sub_start[sub], 16), sub_rows[sub]
            send, recv = entry_plan[sub], weight_slot[(0, sub)]
        else:
            start, size = rest_start[name[1]], rest_rows[name[1]]
            send, recv = rest_plan[name[1]], rest_slots[name[1]]
        return pltpu.make_async_remote_copy(
            src_ref=weight_hbm.at[pl.ds(start, size), :], dst_ref=part_rows(name),
            send_sem=weight_send.at[send], recv_sem=weight_recv.at[recv],
            device_id=pair_target, device_id_type=mesh_ids)

    def weight_relay(d, sub, link):
        landing = weight_landing(d, link)
        return pltpu.make_async_remote_copy(
            src_ref=part_rows(("W", d, sub)), dst_ref=part_rows(("W", landing, sub)),
            send_sem=weight_send.at[weight_plan[((d, sub), link)]], recv_sem=weight_recv.at[weight_slot[(landing, sub)]],
            device_id=z_target(1 if link == "up" else 3), device_id_type=mesh_ids)

    def row_index(group):
        return group[0] * side + group[1]

    def piece_copy(group, piece, link):
        landing = row_index(row_landing(*group, link))
        start = piece * piece_rows
        there = start + (cap if link == "partner" else 0)
        recv = (partner_recv if link == "partner" else row_recv).at[landing * pieces + piece]
        return pltpu.make_async_remote_copy(
            src_ref=rows.at[row_index(group), pl.ds(start, piece_rows), :],
            dst_ref=rows.at[landing, pl.ds(there, piece_rows), :],
            send_sem=row_send.at[row_plan[(group, piece, link)]], recv_sem=recv,
            device_id=row_target(link), device_id_type=mesh_ids)

    def tag_copy(group, link):
        landing = row_index(row_landing(*group, link)) * 2 + (1 if link == "partner" else 0)
        return pltpu.make_async_remote_copy(
            src_ref=tags.at[row_index(group) * 2], dst_ref=tags.at[landing],
            send_sem=tag_send.at[tag_plan[(group, link)]], recv_sem=tag_recv.at[landing],
            device_id=row_target(link), device_id_type=mesh_ids)

    def tag_here(landing):
        return pltpu.make_async_copy(tags.at[landing], tags.at[landing], tag_recv.at[landing])

    def send_onward(p, dy, piece):
        taken = row_links(p, dy, piece) + ["partner"]
        for link in taken:
            piece_copy((p, dy), piece, link).start()
        if piece == 0:
            for link in taken:
                tag_copy((p, dy), link).start()

    entry_copy(entries[0]).start()
    for piece in (0, 2, 1, 3):
        send_onward(0, 0, piece)
    for name in entries[1:]:
        entry_copy(name).start()

    def arrival(event):
        if event[0] == "D":
            here = part_rows(event)
            pltpu.make_async_copy(here, here, weight_recv.at[rest_slots[event[1]]]).wait()
        elif event[0] == "W":
            here = part_rows(event)
            pltpu.make_async_copy(here, here, weight_recv.at[weight_slot[event[1:]]]).wait()
            for link in weight_links(*event[1:]):
                weight_relay(event[1], event[2], link).start()
        else:
            group, piece = event[1:3], event[3]
            here = rows.at[row_index(group), pl.ds(piece * piece_rows, piece_rows), :]
            pltpu.make_async_copy(here, here, row_recv.at[row_index(group) * pieces + piece]).wait()
            if piece == 0:
                tag_here(row_index(group) * 2).wait()
            send_onward(*group, piece)

    my_place = (chip_y * 2 + side_x) * 2 + core

    def stat_copy(group, other):
        return pltpu.make_async_remote_copy(
            src_ref=running.at[row_index(group), other], dst_ref=stats_in.at[my_place],
            send_sem=stat_send.at[row_index(group) * 2 + other], recv_sem=stat_recv,
            device_id=(req, group_owner(group, other)), device_id_type=mesh_ids)

    own_first = me * columns
    pair_first = vocab_id(pair_x, chip_y, core) * columns
    own_blocks = [(0, columns, own_first)]

    def part_blocks(part):
        blocks = []
        for name in parts[part]:
            start = part_place[name][1]
            if name[0] == "W":
                first = lax.rem(req + name[1], side) * quarter + sub_start[name[2]]
                blocks.append((start, sub_rows[name[2]], pair_first + first))
            else:
                blocks.append((start, rest_rows[name[1]], pair_first + rest_start[name[1]]))
        return blocks

    def tile(group, weight_ref, blocks, fresh):
        logits = lax.dot_general(weight_ref[...], rows[group], (((1,), (1,)), ((), ())), preferred_element_type=f32)
        for other in range(2):
            piece = logits[:, other * cap:(other + 1) * cap]
            tag = tags[group * 2 + other]
            peak = jnp.max(piece, axis=0, keepdims=True)
            shifted = piece - peak
            exponent = jnp.exp(shifted)
            total = jnp.sum(exponent, axis=0, keepdims=True)
            spread = jnp.sum(exponent * shifted, axis=0, keepdims=True)
            picked = jnp.zeros((1, cap), f32)
            for start, size, first in blocks:
                column = lax.broadcasted_iota(jnp.int32, (size, cap), 0)
                block = piece[start:start + size]
                picked = picked + jnp.sum(jnp.where(column == tag - first, block, 0.0), axis=0, keepdims=True)
            if not fresh:
                before = running[group, other]
                joint = jnp.maximum(before[0:1], peak)
                drop_before = before[0:1] - joint
                drop = peak - joint
                factor_before = jnp.exp(drop_before)
                factor = jnp.exp(drop)
                spread = factor_before * (before[2:3] + drop_before * before[1:2]) + factor * (spread + drop * total)
                total = factor_before * before[1:2] + factor * total
                picked = picked + before[3:4]
                peak = joint
            running[group, other] = jnp.concatenate([peak, total, spread, picked] * 2, axis=0)

    def at_step(step, index):
        for event in steps[index][0]:
            arrival(event)
        if index == last_own_step + 1:
            pl.semaphore_signal(token_x, inc=1, device_id=pair_target, device_id_type=mesh_ids)
        if index == len(steps) - 3:
            pl.semaphore_wait(token_x, 1)
            for ahead in range(1, side):
                pl.semaphore_signal(token_z, inc=1, device_id=z_target(ahead), device_id_type=mesh_ids)

    busy_steps = [index for index in range(len(steps))
                  if steps[index][0] or index in (last_own_step + 1, len(steps) - 3)]

    def dispatch(step, low, high):
        inside = [index for index in busy_steps if low <= index < high]
        if not inside:
            return
        if len(inside) == 1:
            @pl.when(step == inside[0])
            def _():
                at_step(step, inside[0])
            return
        middle = inside[len(inside) // 2]

        @pl.when(step < middle)
        def _():
            dispatch(step, low, middle)

        @pl.when(step >= middle)
        def _():
            dispatch(step, middle, high)

    def one_step(step, carry):
        dispatch(step, 0, len(steps))
        code = jnp.int32(0)
        for index, (events, kind, group) in enumerate(steps):
            code = jnp.where(step == index, kind * group_count + group, code)
        kind_now = code // group_count
        group_now = lax.rem(code, group_count)

        @pl.when(kind_now == 0)
        def _():
            for piece in range(pieces):
                there = rows.at[group_now, pl.ds(cap + piece * piece_rows, piece_rows), :]
                pltpu.make_async_copy(there, there, partner_recv.at[group_now * pieces + piece]).wait()
            tag_here(group_now * 2 + 1).wait()
            tile(group_now, weight_t, own_blocks, True)

        @pl.when(kind_now > 0)
        def _():
            for part in range(len(parts)):
                @pl.when(kind_now == part + 1)
                def _():
                    tile(group_now, pair_parts[part], part_blocks(part), False)
                    if part + 1 == last_part:
                        where = (group_now // side, lax.rem(group_now, side))
                        stat_copy(where, 1).start()

                        @pl.when(group_now == 0)
                        def _():
                            stats_in[my_place] = running[0, 0]

                        @pl.when(group_now > 0)
                        def _():
                            stat_copy(where, 0).start()
        return carry

    weight_copy.wait()
    lax.fori_loop(0, len(steps), one_step, 0)

    sources = 2 * group_count
    pltpu.make_async_copy(stats_in.at[pl.ds(0, sources - 1)], stats_in.at[pl.ds(0, sources - 1)], stat_recv).wait()

    peak = stats_in[0]
    for index in range(1, sources):
        peak = jnp.maximum(peak, stats_in[index])
    peak = peak[0:1]
    row_total = jnp.zeros((1, cap), f32)
    spread = jnp.zeros((1, cap), f32)
    picked = jnp.zeros((1, cap), f32)
    for index in range(sources):
        stat = stats_in[index]
        below = stat[0:1] - peak
        factor = jnp.exp(below)
        row_total = row_total + stat[1:2] * factor
        spread = spread + factor * (stat[2:3] + below * stat[1:2])
        picked = picked + stat[3:4]
    log_total = jnp.log(row_total)
    logprob = jnp.broadcast_to(picked - peak - log_total, (seq_count, cap))
    entropy = jnp.broadcast_to(log_total - spread / row_total, (seq_count, cap))

    request = lax.broadcasted_iota(jnp.int32, (seq_count, cap), 0)
    lane = lax.broadcasted_iota(jnp.int32, (seq_count, cap), 1)
    offset = jnp.zeros((seq_count, cap), jnp.int32)
    length = jnp.zeros((seq_count, cap), jnp.int32)
    for seq in range(seq_count):
        offset = jnp.where(request == seq, offsets[seq], offset)
        length = jnp.where(request == seq, lens[seq], length)
    bit = 1
    while bit < cap:
        moved = (offset & bit) != 0
        logprob = jnp.where(moved, pltpu.roll(logprob, cap - bit, 1), logprob)
        entropy = jnp.where(moved, pltpu.roll(entropy, cap - bit, 1), entropy)
        bit *= 2
    logprob = jnp.where(lane < length, logprob, 0.0)
    entropy = jnp.where(lane < length, entropy, 0.0)
    both = logprob + pltpu.roll(entropy, seq_len, 1)
    half = seq_count // 2
    mine = req * members + me
    fin[mine] = both[:half] + pltpu.roll(both[half:], cap // 2, 1)

    pl.semaphore_wait(token_z, side - 1)

    def fin_copy(step):
        other = lax.rem(mine + step, members * side)
        return pltpu.make_async_remote_copy(
            src_ref=fin.at[mine], dst_ref=fin.at[mine], send_sem=fin_send, recv_sem=fin_recv,
            device_id=(other // members, lax.rem(other, members)), device_id_type=mesh_ids)

    def send_fin(step, carry):
        fin_copy(step).start()
        return carry

    lax.fori_loop(1, members * side, send_fin, 0)
    others = fin.at[pl.ds(0, members * side - 1)]
    pltpu.make_async_copy(others, others, fin_recv).wait()

    for seq in range(seq_count):
        wanted = slots[seq]
        owner = lax.div(wanted, seq_count)
        inside = lax.rem(wanted, seq_count)
        found = fin[owner]
        turned = pltpu.roll(found, cap // 2, 1)
        found = jnp.where(inside >= half, turned, found)
        level = lax.rem(inside, half)
        row = lax.broadcasted_iota(jnp.int32, (half, cap), 0)
        gathered[pl.ds(seq, 1), :] = jnp.sum(jnp.where(row == level, found, 0.0), axis=0, keepdims=True)
    out[0] = gathered[:, 0:seq_len]
    out[1] = gathered[:, seq_len:2 * seq_len]

    def drain(index, carry):
        here = rows.at[0, pl.ds(0, piece_rows), :]
        pltpu.make_async_copy(here, here, row_send.at[index]).wait()
        return carry

    lax.fori_loop(0, len(row_plan), drain, 0)
    for (d, sub), link in weight_plan:
        weight_relay(d, sub, link).wait_send()
    for name in entries:
        entry_copy(name).wait_send()

    def drain_tags(index, carry):
        pltpu.make_async_copy(tags.at[0], tags.at[0], tag_send.at[index]).wait()
        return carry

    lax.fori_loop(0, len(tag_plan), drain_tags, 0)

    def drain_stats(index, carry):
        pltpu.make_async_copy(stats_in.at[0], stats_in.at[0], stat_send.at[index]).wait()
        return carry

    lax.fori_loop(1, sources, drain_stats, 0)
    pltpu.make_async_copy(others, others, fin_send).wait()


def local(hidden_states, norm_gain, head_weight, targets, lengths, slot_of):
    held, depth = hidden_states.shape
    seq_count = lengths.shape[0]
    seq_len = held // seq_count
    columns = head_weight.shape[1]
    members = 2 * side * side
    vmem = pl.BlockSpec(memory_space=pltpu.VMEM)
    smem = pl.BlockSpec(memory_space=pltpu.SMEM)
    dma = pltpu.SemaphoreType.DMA
    regular = pltpu.SemaphoreType.REGULAR
    out = jax.ShapeDtypeStruct((2, seq_count, seq_len), f32)
    both = pl.pallas_call(
        kernel,
        out_shape=out,
        in_specs=[smem, smem, vmem, vmem, vmem, pl.BlockSpec(memory_space=pl.ANY)],
        out_specs=vmem,
        scratch_shapes=[
            pltpu.VMEM((columns, depth), jnp.bfloat16),
            pltpu.VMEM((group_count, 2 * cap, depth), jnp.bfloat16),
            pltpu.VMEM((2 * group_count, 1, cap), jnp.int32),
            pltpu.VMEM((group_count, 2, 8, cap), f32),
            pltpu.VMEM((2 * group_count, 8, cap), f32),
            pltpu.VMEM((members * side, seq_count // 2, cap), f32),
            pltpu.VMEM((seq_count, cap), f32),
        ] + [pltpu.VMEM((size, depth), jnp.bfloat16) for size in part_sizes] + [
            dma,
            dma((len(row_plan),)),
            dma((group_count * pieces,)),
            dma((group_count * pieces,)),
            dma((weight_sends,)),
            dma((rest_slots[-1] + 1,)),
            dma((len(tag_plan),)),
            dma((2 * group_count,)),
            dma((2 * group_count,)),
            dma,
            regular,
            regular,
            dma,
            dma,
        ],
        compiler_params=pltpu.CompilerParams(collective_id=0, has_side_effects=True, vmem_limit_bytes=60 << 20),
        name="head_stats",
    )(lengths, slot_of, hidden_states, norm_gain.reshape(1, depth), targets.reshape(1, held), head_weight.T)
    return (both[0], both[1])


def solution(mesh):
    rows = jax.sharding.PartitionSpec(("req", "vocab"), None)
    flat = jax.sharding.PartitionSpec(("req", "vocab"))
    in_specs = (rows, jax.sharding.PartitionSpec(), jax.sharding.PartitionSpec(None, "vocab"), flat, flat, flat)
    return jax.shard_map(local, mesh=mesh, in_specs=in_specs, out_specs=(rows, rows), check_vma=False)
```

```python
import jax
import jax.numpy as jnp
from jax import lax
from jax.experimental import pallas as pl
from jax.experimental.pallas import tpu as pltpu

eps_norm = 1e-05
side = 4
cap = 128
pieces = 4
piece_rows = cap // pieces
group_count = 2 * side
mesh_ids = pl.DeviceIdType.MESH
f32 = jnp.float32

sub_rows = (32, 32, 16, 32, 64, 32)
rest_rows = (80, 88)
entries = [("W", 0, 0), ("W", 0, 1), ("W", 0, 2), ("W", 0, 3), ("W", 0, 4), ("W", 0, 5), ("D", 0), ("D", 1)]
parts = [[("W", 0, 0), ("W", 0, 1), ("W", 0, 2), ("W", 3, 0), ("W", 1, 0), ("W", 0, 3), ("W", 3, 1), ("W", 1, 1), ("W", 3, 2), ("W", 1, 2), ("W", 2, 0), ("W", 1, 3), ("W", 0, 4), ("W", 3, 3), ("W", 2, 1), ("W", 0, 5)], [("W", 2, 2), ("W", 2, 3), ("W", 3, 4), ("D", 0), ("W", 1, 4), ("W", 3, 5), ("W", 1, 5), ("W", 2, 4), ("W", 2, 5), ("D", 1)]]
steps = [
    ([("W", 0, 0), ("R", 1, 0, 0), ("R", 0, 3, 0), ("R", 0, 1, 0), ("W", 0, 1), ("R", 0, 3, 2), ("R", 0, 1, 2), ("R", 1, 0, 2), ("W", 0, 2), ("W", 3, 0), ("W", 1, 0), ("R", 1, 0, 1), ("R", 0, 3, 1), ("R", 0, 1, 1), ("W", 0, 3), ("W", 3, 1), ("W", 1, 1), ("R", 0, 3, 3), ("R", 0, 1, 3), ("R", 1, 0, 3), ("W", 3, 2), ("W", 1, 2)], 0, 0),
    ([("R", 1, 3, 0), ("R", 1, 1, 0), ("R", 1, 3, 2)], 0, 1),
    ([("W", 2, 0), ("W", 1, 3), ("W", 0, 4)], 1, 0),
    ([("R", 0, 2, 0), ("R", 1, 1, 2), ("R", 1, 1, 1), ("W", 3, 3), ("W", 2, 1)], 1, 1),
    ([("W", 0, 5), ("W", 2, 2)], 2, 0),
    ([("R", 0, 2, 2), ("R", 0, 2, 1), ("R", 1, 3, 3), ("W", 2, 3)], 2, 1),
    ([("R", 1, 3, 1), ("R", 1, 1, 3), ("R", 0, 2, 3)], 0, 2),
    ([("W", 3, 4), ("D", 0), ("R", 1, 2, 0), ("R", 1, 2, 1), ("R", 1, 2, 2)], 1, 2),
    ([("W", 1, 4), ("W", 3, 5)], 2, 2),
    ([("R", 1, 2, 3), ("W", 1, 5)], 0, 3),
    ([], 1, 3),
    ([("W", 2, 4)], 2, 3),
    ([("W", 2, 5), ("D", 1)], 3, 3),
    ([], 3, 2),
    ([], 3, 1),
    ([], 3, 0),
]
sub_start = [sum(sub_rows[:index]) for index in range(len(sub_rows))]
quarter = sum(sub_rows)
part_place = {}
part_sizes = []
for part_index, part_list in enumerate(parts):
    filled = 0
    for part_piece in part_list:
        part_place[part_piece] = (part_index, filled)
        filled += sub_rows[part_piece[2]] if part_piece[0] == "W" else rest_rows[part_piece[1]]
    part_sizes.append(filled)
rest_start = [side * quarter + sum(rest_rows[:index]) for index in range(len(rest_rows))]


def row_links(p, dy, q):
    taken = []
    x_first = q < 2
    upward = q % 2 == 0
    if x_first:
        if (p, dy) == (0, 0):
            taken.append("x")
        if dy == 0:
            taken += ["up", "down"]
    else:
        if (p, dy) == (0, 0):
            taken += ["up", "down"]
        if p == 0:
            taken.append("x")
    if x_first or p == 0:
        if dy == 3 and upward:
            taken.append("up")
        if dy == 1 and not upward:
            taken.append("down")
    return taken


def row_landing(p, dy, link):
    if link == "x":
        return (1 - p, dy)
    if link == "partner":
        return (p, dy)
    return (p, (dy + (3 if link == "up" else 1)) % side)


def weight_links(d, sub):
    if d == 0:
        return ["up", "down"]
    if d == 3 and sub % 2 == 0:
        return ["up"]
    if d == 1 and sub % 2 == 1:
        return ["down"]
    return []


def weight_landing(d, link):
    return (d + (3 if link == "up" else 1)) % side


all_groups = [(0, 0), (0, 1), (0, 3), (1, 0), (1, 1), (1, 3), (0, 2), (1, 2)]
row_plan = {}
tag_plan = {}
tag_first = {}
for plan_group in all_groups:
    for plan_link in ["partner", "x", "up", "down"]:
        for plan_piece in range(pieces):
            if plan_link == "partner" or plan_link in row_links(*plan_group, plan_piece):
                row_plan[(plan_group, plan_piece, plan_link)] = len(row_plan)
                landing_group = row_landing(*plan_group, plan_link)
                if plan_piece == 0:
                    tag_plan[(plan_group, plan_link)] = len(tag_plan)
weight_arrivals = [(d, sub) for d in range(side) for sub in range(len(sub_rows))]
weight_slot = {arrival: index for index, arrival in enumerate(weight_arrivals)}
rest_slots = [len(weight_arrivals) + index for index in range(len(rest_rows))]
weight_plan = {}
for plan_arrival in weight_arrivals:
    for plan_link in weight_links(*plan_arrival):
        weight_plan[(plan_arrival, plan_link)] = len(weight_plan)
entry_plan = {sub: len(weight_plan) + sub for sub in range(len(sub_rows))}
rest_plan = [len(weight_plan) + len(sub_rows) + index for index in range(len(rest_rows))]
weight_sends = rest_plan[-1] + 1
part_count = 2 + len(parts)
last_own_step = max(index for index, step_entry in enumerate(steps) if step_entry[1] == 0)


def kernel(lens, slots, hidden, gain, targets, weight_hbm, out, *scratch):
    (weights, column_ids, rows, tags, running, stats_in, fin, gathered, weight_sem, row_send, row_recv, partner_recv, weight_send, weight_recv, tag_send, tag_recv,
     stat_send, stat_recv, token_x, token_z, fin_send, fin_recv) = scratch
    req = lax.axis_index("req")
    me = lax.axis_index("vocab")
    core = lax.rem(me, 2)
    chip_x = lax.rem(me // 2, side)
    chip_y = me // (2 * side)
    members = 2 * side * side
    columns, depth = weight_hbm.shape
    part_height = weights.shape[1]
    own_sizes = (part_height, columns - part_height)
    side_x = lax.rem(chip_x, 2)
    pair_x = side - 1 - chip_x

    def vocab_id(x, y, the_core):
        return (y * side + x) * 2 + the_core

    def group_owner(group, other):
        p, dy = group
        x = chip_x + p * (1 - 2 * side_x)
        return vocab_id(x, lax.rem(chip_y + dy, side), (1 - core) if other else core)

    def row_target(link):
        if link == "partner":
            return (req, vocab_id(chip_x, chip_y, 1 - core))
        if link == "x":
            return (req, group_owner((1, 0), False))
        return (req, group_owner((0, 1 if link == "up" else 3), False))

    def z_target(ahead):
        return (lax.rem(req + ahead, side), me)

    pair_target = (req, vocab_id(pair_x, chip_y, core))

    barrier = pltpu.get_barrier_semaphore()
    neighbours = [row_target(link) for link in ("partner", "x", "up", "down")] + [pair_target, z_target(1), z_target(3)]
    for neighbour in neighbours:
        pl.semaphore_signal(barrier, inc=1, device_id=neighbour, device_id_type=mesh_ids)

    def own_copy(part):
        return pltpu.make_async_copy(
            weight_hbm.at[pl.ds(part * part_height, own_sizes[part]), :],
            weights.at[part, pl.ds(0, own_sizes[part]), :], weight_sem.at[part])

    for part in range(2):
        own_copy(part).start()

    seq_count = lens.shape[0]
    held = hidden.shape[0]
    seq_len = held // seq_count
    offsets = []
    total_length = jnp.int32(0)
    for seq in range(seq_count):
        offsets.append(total_length)
        total_length = total_length + lens[seq]

    def compact_place(slot_index):
        place = jnp.full(slot_index.shape, -1, jnp.int32)
        for seq in range(seq_count):
            ahead = slot_index - seq * seq_len
            place = jnp.where((ahead >= 0) & (ahead < lens[seq]), ahead + offsets[seq], place)
        return place

    place_row = compact_place(lax.broadcasted_iota(jnp.int32, (8, held), 1))[:1]
    pick = (lax.broadcasted_iota(jnp.int32, (cap, held), 0) == place_row).astype(f32).astype(jnp.bfloat16)
    live = jnp.dot(pick, hidden[...], preferred_element_type=f32)
    inverse_rms = lax.rsqrt(jnp.mean(live * live, axis=1, keepdims=True) + eps_norm)
    rows[0, 0:cap, :] = (live * inverse_rms * gain[...]).astype(jnp.bfloat16)

    place_col = compact_place(lax.broadcasted_iota(jnp.int32, (held, cap), 0))
    pick_t = (lax.broadcasted_iota(jnp.int32, (held, cap), 1) == place_col).astype(f32).astype(jnp.bfloat16)
    wide = targets[...]
    high = wide // 256
    digits = jnp.concatenate([high, wide - high * 256] + [jnp.zeros_like(wide)] * 14, axis=0)
    digits = digits.astype(f32).astype(jnp.bfloat16)
    tag_pair = jnp.dot(digits, pick_t, preferred_element_type=f32)
    tags[0] = (tag_pair[0:1] * 256.0 + tag_pair[1:2]).astype(jnp.int32)

    pl.semaphore_wait(barrier, len(neighbours))

    def part_rows(arrival_name):
        part, start = part_place[arrival_name]
        size = sub_rows[arrival_name[2]] if arrival_name[0] == "W" else rest_rows[arrival_name[1]]
        return weights.at[2 + part, pl.ds(start, size), :]

    def entry_copy(name):
        if name[0] == "W":
            sub = name[2]
            start, size = pl.multiple_of(req * quarter + sub_start[sub], 16), sub_rows[sub]
            send, recv = entry_plan[sub], weight_slot[(0, sub)]
        else:
            start, size = rest_start[name[1]], rest_rows[name[1]]
            send, recv = rest_plan[name[1]], rest_slots[name[1]]
        return pltpu.make_async_remote_copy(
            src_ref=weight_hbm.at[pl.ds(start, size), :], dst_ref=part_rows(name),
            send_sem=weight_send.at[send], recv_sem=weight_recv.at[recv],
            device_id=pair_target, device_id_type=mesh_ids)

    def weight_relay(d, sub, link):
        landing = weight_landing(d, link)
        return pltpu.make_async_remote_copy(
            src_ref=part_rows(("W", d, sub)), dst_ref=part_rows(("W", landing, sub)),
            send_sem=weight_send.at[weight_plan[((d, sub), link)]], recv_sem=weight_recv.at[weight_slot[(landing, sub)]],
            device_id=z_target(1 if link == "up" else 3), device_id_type=mesh_ids)

    def row_index(group):
        return all_groups.index(group)

    def piece_copy(group, piece, link):
        landing = row_index(row_landing(*group, link))
        start = piece * piece_rows
        there = start + (cap if link == "partner" else 0)
        recv = (partner_recv if link == "partner" else row_recv).at[landing * pieces + piece]
        return pltpu.make_async_remote_copy(
            src_ref=rows.at[row_index(group), pl.ds(start, piece_rows), :],
            dst_ref=rows.at[landing, pl.ds(there, piece_rows), :],
            send_sem=row_send.at[row_plan[(group, piece, link)]], recv_sem=recv,
            device_id=row_target(link), device_id_type=mesh_ids)

    def tag_copy(group, link):
        landing = row_index(row_landing(*group, link)) * 2 + (1 if link == "partner" else 0)
        return pltpu.make_async_remote_copy(
            src_ref=tags.at[row_index(group) * 2], dst_ref=tags.at[landing],
            send_sem=tag_send.at[tag_plan[(group, link)]], recv_sem=tag_recv.at[landing],
            device_id=row_target(link), device_id_type=mesh_ids)

    def tag_here(landing):
        return pltpu.make_async_copy(tags.at[landing], tags.at[landing], tag_recv.at[landing])

    def send_onward(p, dy, piece):
        taken = row_links(p, dy, piece) + ["partner"]
        for link in taken:
            piece_copy((p, dy), piece, link).start()
        if piece == 0:
            for link in taken:
                tag_copy((p, dy), link).start()

    entry_copy(entries[0]).start()
    for piece in (0, 2, 1, 3):
        send_onward(0, 0, piece)
    for name in entries[1:]:
        entry_copy(name).start()

    def arrival(event):
        if event[0] == "D":
            here = part_rows(event)
            pltpu.make_async_copy(here, here, weight_recv.at[rest_slots[event[1]]]).wait()
        elif event[0] == "W":
            here = part_rows(event)
            pltpu.make_async_copy(here, here, weight_recv.at[weight_slot[event[1:]]]).wait()
            for link in weight_links(*event[1:]):
                weight_relay(event[1], event[2], link).start()
        else:
            group, piece = event[1:3], event[3]
            here = rows.at[row_index(group), pl.ds(piece * piece_rows, piece_rows), :]
            pltpu.make_async_copy(here, here, row_recv.at[row_index(group) * pieces + piece]).wait()
            if piece == 0:
                tag_here(row_index(group) * 2).wait()
            send_onward(*group, piece)

    my_place = (chip_y * 2 + side_x) * 2 + core

    def stat_copy(slot, group, other):
        return pltpu.make_async_remote_copy(
            src_ref=running.at[slot, other], dst_ref=stats_in.at[my_place],
            send_sem=stat_send.at[slot * 2 + other], recv_sem=stat_recv,
            device_id=(req, group_owner(group, other)), device_id_type=mesh_ids)

    own_first = me * columns
    pair_first = vocab_id(pair_x, chip_y, core) * columns

    def part_blocks(part):
        if part < 2:
            return [(0, own_sizes[part], own_first + part * part_height)]
        blocks = []
        for name in parts[part - 2]:
            start = part_place[name][1]
            if name[0] == "W":
                first = lax.rem(req + name[1], side) * quarter + sub_start[name[2]]
                blocks.append((start, sub_rows[name[2]], pair_first + first))
            else:
                blocks.append((start, rest_rows[name[1]], pair_first + rest_start[name[1]]))
        return blocks

    for part in range(part_count):
        filled = 0
        for start, size, first in part_blocks(part):
            column_ids[part, pl.ds(start, size), :] = lax.broadcasted_iota(jnp.int32, (size, cap), 0) + first
            filled += size
        if filled < part_height:
            missing = part_height - filled
            column_ids[part, pl.ds(filled, missing), :] = jnp.full((missing, cap), -1, jnp.int32)
            weights[part, pl.ds(filled, missing), :] = jnp.zeros((missing, depth), jnp.bfloat16)
    empty = jnp.where(lax.rem(lax.broadcasted_iota(jnp.int32, (8, cap), 0), 4) == 0, -1e30, 0.0)
    for group in range(group_count):
        for other in range(2):
            running[group, other] = empty

    sure = part_height - 8

    def tile(pair, part):
        taken = rows[pl.ds(pair * 2, 2)].reshape(4 * cap, depth)
        logits = lax.dot_general(weights[part], taken, (((1,), (1,)), ((), ())), preferred_element_type=f32)
        for block_index in range(4):
            group = pair * 2 + block_index // 2
            other = block_index % 2
            lanes = slice(block_index * cap, (block_index + 1) * cap)
            tag = tags[group * 2 + other]
            ids_tail = column_ids[part, sure:, :]
            main = logits[:sure, lanes]
            tail = jnp.where(ids_tail >= 0, logits[sure:, lanes], -1e30)
            peak = jnp.max(jnp.maximum(jnp.max(main.reshape(sure // 8, 8, cap), axis=0), tail), axis=0, keepdims=True)
            shifted = main - peak
            exponent = jnp.exp(shifted)
            shifted_tail = tail - peak
            exponent_tail = jnp.exp(shifted_tail)
            chosen = jnp.where(column_ids[part, :sure, :] == tag, main, 0.0)
            chosen_tail = jnp.where(ids_tail == tag, tail, 0.0)

            def summed(many, few):
                return jnp.sum(jnp.sum(many.reshape(sure // 8, 8, cap), axis=0) + few, axis=0, keepdims=True)

            total = summed(exponent, exponent_tail)
            spread = summed(exponent * shifted, exponent_tail * shifted_tail)
            picked = summed(chosen, chosen_tail)
            before = running[group, other]
            joint = jnp.maximum(before[0:1], peak)
            drop_before = before[0:1] - joint
            drop = peak - joint
            factor_before = jnp.exp(drop_before)
            factor = jnp.exp(drop)
            spread = factor_before * (before[2:3] + drop_before * before[1:2]) + factor * (spread + drop * total)
            total = factor_before * before[1:2] + factor * total
            running[group, other] = jnp.concatenate([joint, total, spread, picked + before[3:4]] * 2, axis=0)

    def at_step(step, index):
        for event in steps[index][0]:
            arrival(event)
        if index == last_own_step + 1:
            pl.semaphore_signal(token_x, inc=1, device_id=pair_target, device_id_type=mesh_ids)
        if index == len(steps) - 3:
            pl.semaphore_wait(token_x, 1)
            for ahead in range(1, side):
                pl.semaphore_signal(token_z, inc=1, device_id=z_target(ahead), device_id_type=mesh_ids)

    busy_steps = [index for index in range(len(steps))
                  if steps[index][0] or index in (last_own_step + 1, len(steps) - 3)]

    def dispatch(step, low, high):
        inside = [index for index in busy_steps if low <= index < high]
        if not inside:
            return
        if len(inside) == 1:
            @pl.when(step == inside[0])
            def _():
                at_step(step, inside[0])
            return
        middle = inside[len(inside) // 2]

        @pl.when(step < middle)
        def _():
            dispatch(step, low, middle)

        @pl.when(step >= middle)
        def _():
            dispatch(step, middle, high)

    def one_step(step, carry):
        dispatch(step, 0, len(steps))
        code = jnp.int32(0)
        for index, (events, part, pair) in enumerate(steps):
            code = jnp.where(step == index, part * side + pair, code)
        part_now = code // side
        pair_now = lax.rem(code, side)

        @pl.when(part_now == 0)
        def _():
            for member in range(2):
                group = pair_now * 2 + member
                for piece in range(pieces):
                    there = rows.at[group, pl.ds(cap + piece * piece_rows, piece_rows), :]
                    pltpu.make_async_copy(there, there, partner_recv.at[group * pieces + piece]).wait()
                tag_here(group * 2 + 1).wait()

        tile(pair_now, part_now)

        @pl.when(part_now == part_count - 1)
        def _():
            for member in range(2):
                slot = pair_now * 2 + member
                p = jnp.int32(0)
                dy = jnp.int32(0)
                for index in range(member, group_count, 2):
                    p = jnp.where(slot == index, all_groups[index][0], p)
                    dy = jnp.where(slot == index, all_groups[index][1], dy)
                stat_copy(slot, (p, dy), 1).start()
                if member == 1:
                    stat_copy(slot, (p, dy), 0).start()
                else:
                    @pl.when(pair_now == 0)
                    def _():
                        stats_in[my_place] = running[0, 0]

                    @pl.when(pair_now > 0)
                    def _():
                        stat_copy(slot, (p, dy), 0).start()
        return carry

    for part in range(2):
        own_copy(part).wait()
    lax.fori_loop(0, len(steps), one_step, 0)

    sources = 2 * group_count
    pltpu.make_async_copy(stats_in.at[pl.ds(0, sources - 1)], stats_in.at[pl.ds(0, sources - 1)], stat_recv).wait()

    peak = stats_in[0]
    for index in range(1, sources):
        peak = jnp.maximum(peak, stats_in[index])
    peak = peak[0:1]
    row_total = jnp.zeros((1, cap), f32)
    spread = jnp.zeros((1, cap), f32)
    picked = jnp.zeros((1, cap), f32)
    for index in range(sources):
        stat = stats_in[index]
        below = stat[0:1] - peak
        factor = jnp.exp(below)
        row_total = row_total + stat[1:2] * factor
        spread = spread + factor * (stat[2:3] + below * stat[1:2])
        picked = picked + stat[3:4]
    log_total = jnp.log(row_total)
    logprob = jnp.broadcast_to(picked - peak - log_total, (seq_count, cap))
    entropy = jnp.broadcast_to(log_total - spread / row_total, (seq_count, cap))

    request = lax.broadcasted_iota(jnp.int32, (seq_count, cap), 0)
    lane = lax.broadcasted_iota(jnp.int32, (seq_count, cap), 1)
    offset = jnp.zeros((seq_count, cap), jnp.int32)
    length = jnp.zeros((seq_count, cap), jnp.int32)
    for seq in range(seq_count):
        offset = jnp.where(request == seq, offsets[seq], offset)
        length = jnp.where(request == seq, lens[seq], length)
    bit = 1
    while bit < cap:
        moved = (offset & bit) != 0
        logprob = jnp.where(moved, pltpu.roll(logprob, cap - bit, 1), logprob)
        entropy = jnp.where(moved, pltpu.roll(entropy, cap - bit, 1), entropy)
        bit *= 2
    logprob = jnp.where(lane < length, logprob, 0.0)
    entropy = jnp.where(lane < length, entropy, 0.0)
    both = logprob + pltpu.roll(entropy, seq_len, 1)
    half = seq_count // 2
    mine = req * members + me
    fin[mine] = both[:half] + pltpu.roll(both[half:], cap // 2, 1)

    pl.semaphore_wait(token_z, side - 1)

    def fin_copy(step):
        other = lax.rem(mine + step, members * side)
        return pltpu.make_async_remote_copy(
            src_ref=fin.at[mine], dst_ref=fin.at[mine], send_sem=fin_send, recv_sem=fin_recv,
            device_id=(other // members, lax.rem(other, members)), device_id_type=mesh_ids)

    def send_fin(step, carry):
        fin_copy(step).start()
        return carry

    lax.fori_loop(1, members * side, send_fin, 0)
    others = fin.at[pl.ds(0, members * side - 1)]
    pltpu.make_async_copy(others, others, fin_recv).wait()

    for seq in range(seq_count):
        wanted = slots[seq]
        owner = lax.div(wanted, seq_count)
        inside = lax.rem(wanted, seq_count)
        found = fin[owner]
        turned = pltpu.roll(found, cap // 2, 1)
        found = jnp.where(inside >= half, turned, found)
        level = lax.rem(inside, half)
        row = lax.broadcasted_iota(jnp.int32, (half, cap), 0)
        gathered[pl.ds(seq, 1), :] = jnp.sum(jnp.where(row == level, found, 0.0), axis=0, keepdims=True)
    out[0] = gathered[:, 0:seq_len]
    out[1] = gathered[:, seq_len:2 * seq_len]

    def drain(index, carry):
        here = rows.at[0, pl.ds(0, piece_rows), :]
        pltpu.make_async_copy(here, here, row_send.at[index]).wait()
        return carry

    lax.fori_loop(0, len(row_plan), drain, 0)
    for (d, sub), link in weight_plan:
        weight_relay(d, sub, link).wait_send()
    for name in entries:
        entry_copy(name).wait_send()

    def drain_tags(index, carry):
        pltpu.make_async_copy(tags.at[0], tags.at[0], tag_send.at[index]).wait()
        return carry

    lax.fori_loop(0, len(tag_plan), drain_tags, 0)

    def drain_stats(index, carry):
        pltpu.make_async_copy(stats_in.at[0], stats_in.at[0], stat_send.at[index]).wait()
        return carry

    lax.fori_loop(1, sources, drain_stats, 0)
    pltpu.make_async_copy(others, others, fin_send).wait()


def local(hidden_states, norm_gain, head_weight, targets, lengths, slot_of):
    held, depth = hidden_states.shape
    seq_count = lengths.shape[0]
    seq_len = held // seq_count
    columns = head_weight.shape[1]
    members = 2 * side * side
    vmem = pl.BlockSpec(memory_space=pltpu.VMEM)
    smem = pl.BlockSpec(memory_space=pltpu.SMEM)
    dma = pltpu.SemaphoreType.DMA
    regular = pltpu.SemaphoreType.REGULAR
    part_height = max(part_sizes + [columns - max(part_sizes)])
    out = jax.ShapeDtypeStruct((2, seq_count, seq_len), f32)
    both = pl.pallas_call(
        kernel,
        out_shape=out,
        in_specs=[smem, smem, vmem, vmem, vmem, pl.BlockSpec(memory_space=pl.ANY)],
        out_specs=vmem,
        scratch_shapes=[
            pltpu.VMEM((part_count, part_height, depth), jnp.bfloat16),
            pltpu.VMEM((part_count, part_height, cap), jnp.int32),
            pltpu.VMEM((group_count, 2 * cap, depth), jnp.bfloat16),
            pltpu.VMEM((2 * group_count, 1, cap), jnp.int32),
            pltpu.VMEM((group_count, 2, 8, cap), f32),
            pltpu.VMEM((2 * group_count, 8, cap), f32),
            pltpu.VMEM((members * side, seq_count // 2, cap), f32),
            pltpu.VMEM((seq_count, cap), f32),
            dma((2,)),
            dma((len(row_plan),)),
            dma((group_count * pieces,)),
            dma((group_count * pieces,)),
            dma((weight_sends,)),
            dma((rest_slots[-1] + 1,)),
            dma((len(tag_plan),)),
            dma((2 * group_count,)),
            dma((2 * group_count,)),
            dma,
            regular,
            regular,
            dma,
            dma,
        ],
        compiler_params=pltpu.CompilerParams(collective_id=0, has_side_effects=True, vmem_limit_bytes=60 << 20),
        name="head_stats",
    )(lengths, slot_of, hidden_states, norm_gain.reshape(1, depth), targets.reshape(1, held), head_weight.T)
    return (both[0], both[1])


def solution(mesh):
    rows = jax.sharding.PartitionSpec(("req", "vocab"), None)
    flat = jax.sharding.PartitionSpec(("req", "vocab"))
    in_specs = (rows, jax.sharding.PartitionSpec(), jax.sharding.PartitionSpec(None, "vocab"), flat, flat, flat)
    return jax.shard_map(local, mesh=mesh, in_specs=in_specs, out_specs=(rows, rows), check_vma=False)
```

```python
import jax
import jax.numpy as jnp
from jax import lax
from jax.experimental import pallas as pl
from jax.experimental.pallas import tpu as pltpu

eps_norm = 1e-05
side = 4
cap = 128
pieces = 4
piece_rows = cap // pieces
group_count = 2 * side
mesh_ids = pl.DeviceIdType.MESH
f32 = jnp.float32

own_part_sizes = (504, 496)
sub_rows = (32, 32, 16, 32, 64, 32)
rest_rows = (80, 88)
entries = [("W", 0, 0), ("W", 0, 1), ("W", 0, 2), ("W", 0, 3), ("W", 0, 4), ("W", 0, 5), ("D", 0), ("D", 1)]
parts = [[("W", 0, 0), ("W", 0, 1), ("W", 0, 2), ("W", 3, 0), ("W", 1, 0), ("W", 0, 3), ("W", 3, 1), ("W", 1, 1), ("W", 3, 2), ("W", 1, 2), ("W", 2, 0), ("W", 1, 3), ("W", 0, 4), ("W", 3, 3), ("W", 2, 1), ("W", 0, 5)], [("W", 2, 2), ("W", 2, 3), ("W", 3, 4), ("D", 0), ("W", 1, 4), ("W", 3, 5), ("W", 1, 5), ("W", 2, 4), ("W", 2, 5), ("D", 1)]]
steps = [
    ([], 0, 4),
    ([], 1, 4),
    ([("W", 0, 0), ("R", 1, 0, 0), ("R", 0, 3, 0), ("R", 0, 1, 0), ("W", 0, 1), ("R", 0, 3, 2), ("R", 0, 1, 2), ("R", 1, 0, 2), ("W", 0, 2), ("W", 3, 0), ("W", 1, 0), ("R", 1, 0, 1), ("R", 0, 3, 1), ("R", 0, 1, 1), ("W", 0, 3), ("W", 3, 1), ("W", 1, 1), ("R", 0, 3, 3), ("R", 0, 1, 3), ("R", 1, 0, 3), ("W", 3, 2), ("W", 1, 2)], 0, 5),
    ([], 0, 1),
    ([("R", 1, 3, 0), ("R", 1, 1, 0), ("R", 1, 3, 2), ("W", 2, 0), ("W", 1, 3)], 1, 5),
    ([("W", 0, 4)], 1, 1),
    ([("R", 0, 2, 0), ("R", 1, 1, 2), ("R", 1, 1, 1), ("W", 3, 3), ("W", 2, 1), ("W", 0, 5)], 2, 0),
    ([("W", 2, 2), ("R", 0, 2, 2), ("R", 0, 2, 1), ("R", 1, 3, 3)], 2, 1),
    ([("W", 2, 3), ("R", 1, 3, 1), ("R", 1, 1, 3), ("R", 0, 2, 3)], 0, 2),
    ([("W", 3, 4), ("D", 0), ("R", 1, 2, 0), ("R", 1, 2, 1), ("R", 1, 2, 2)], 1, 2),
    ([("W", 1, 4), ("W", 3, 5)], 2, 2),
    ([("R", 1, 2, 3), ("W", 1, 5)], 0, 3),
    ([], 1, 3),
    ([("W", 2, 4)], 2, 3),
    ([("W", 2, 5), ("D", 1)], 3, 3),
    ([], 3, 2),
    ([], 3, 1),
    ([], 3, 0),
]
sub_start = [sum(sub_rows[:index]) for index in range(len(sub_rows))]
quarter = sum(sub_rows)
part_place = {}
part_sizes = []
for part_index, part_list in enumerate(parts):
    filled = 0
    for part_piece in part_list:
        part_place[part_piece] = (part_index, filled)
        filled += sub_rows[part_piece[2]] if part_piece[0] == "W" else rest_rows[part_piece[1]]
    part_sizes.append(filled)
rest_start = [side * quarter + sum(rest_rows[:index]) for index in range(len(rest_rows))]


def row_links(p, dy, q):
    taken = []
    x_first = q < 2
    upward = q % 2 == 0
    if x_first:
        if (p, dy) == (0, 0):
            taken.append("x")
        if dy == 0:
            taken += ["up", "down"]
    else:
        if (p, dy) == (0, 0):
            taken += ["up", "down"]
        if p == 0:
            taken.append("x")
    if x_first or p == 0:
        if dy == 3 and upward:
            taken.append("up")
        if dy == 1 and not upward:
            taken.append("down")
    return taken


def row_landing(p, dy, link):
    if link == "x":
        return (1 - p, dy)
    if link == "partner":
        return (p, dy)
    return (p, (dy + (3 if link == "up" else 1)) % side)


def weight_links(d, sub):
    if d == 0:
        return ["up", "down"]
    if d == 3 and sub % 2 == 0:
        return ["up"]
    if d == 1 and sub % 2 == 1:
        return ["down"]
    return []


def weight_landing(d, link):
    return (d + (3 if link == "up" else 1)) % side


all_groups = [(0, 0), (0, 1), (0, 3), (1, 0), (1, 1), (1, 3), (0, 2), (1, 2)]
row_plan = {}
tag_plan = {}
tag_first = {}
for plan_group in all_groups:
    for plan_link in ["partner", "x", "up", "down"]:
        for plan_piece in range(pieces):
            if plan_link == "partner" or plan_link in row_links(*plan_group, plan_piece):
                row_plan[(plan_group, plan_piece, plan_link)] = len(row_plan)
                landing_group = row_landing(*plan_group, plan_link)
                if plan_piece == 0:
                    tag_plan[(plan_group, plan_link)] = len(tag_plan)
weight_arrivals = [(d, sub) for d in range(side) for sub in range(len(sub_rows))]
weight_slot = {arrival: index for index, arrival in enumerate(weight_arrivals)}
rest_slots = [len(weight_arrivals) + index for index in range(len(rest_rows))]
weight_plan = {}
for plan_arrival in weight_arrivals:
    for plan_link in weight_links(*plan_arrival):
        weight_plan[(plan_arrival, plan_link)] = len(weight_plan)
entry_plan = {sub: len(weight_plan) + sub for sub in range(len(sub_rows))}
rest_plan = [len(weight_plan) + len(sub_rows) + index for index in range(len(rest_rows))]
weight_sends = rest_plan[-1] + 1
own_sizes = own_part_sizes
own_parts = len(own_sizes)
part_count = own_parts + len(parts)
part_height = max(own_sizes + tuple(part_sizes))
ragged = part_height - min(own_sizes + tuple(part_sizes))
last_own_step = max(index for index, step_entry in enumerate(steps) if step_entry[1] == 0)


def kernel(lens, slots, hidden, gain, targets, weight_hbm, out, *scratch):
    (hidden_here, gain_here, targets_here, input_sem, weights, column_ids, rows, tags, running, stats_in, fin, gathered, weight_sem, row_send, row_recv, partner_recv, weight_send, weight_recv, tag_send, tag_recv,
     stat_send, stat_recv, token_x, token_z, fin_send, fin_recv) = scratch
    input_copies = [pltpu.make_async_copy(source, target, input_sem.at[index]) for index, (source, target) in enumerate(
        [(hidden, hidden_here), (gain, gain_here), (targets, targets_here)])]
    for input_copy in input_copies:
        input_copy.start()
    req = lax.axis_index("req")
    me = lax.axis_index("vocab")
    core = lax.rem(me, 2)
    chip_x = lax.rem(me // 2, side)
    chip_y = me // (2 * side)
    members = 2 * side * side
    columns, depth = weight_hbm.shape
    side_x = lax.rem(chip_x, 2)
    pair_x = side - 1 - chip_x

    def vocab_id(x, y, the_core):
        return (y * side + x) * 2 + the_core

    def group_owner(group, other):
        p, dy = group
        x = chip_x + p * (1 - 2 * side_x)
        return vocab_id(x, lax.rem(chip_y + dy, side), (1 - core) if other else core)

    def row_target(link):
        if link == "partner":
            return (req, vocab_id(chip_x, chip_y, 1 - core))
        if link == "x":
            return (req, group_owner((1, 0), False))
        return (req, group_owner((0, 1 if link == "up" else 3), False))

    def z_target(ahead):
        return (lax.rem(req + ahead, side), me)

    pair_target = (req, vocab_id(pair_x, chip_y, core))

    barrier = pltpu.get_barrier_semaphore()
    neighbours = [row_target(link) for link in ("partner", "x", "up", "down")] + [pair_target, z_target(1), z_target(3)]
    for neighbour in neighbours:
        pl.semaphore_signal(barrier, inc=1, device_id=neighbour, device_id_type=mesh_ids)

    def own_copy(part):
        return pltpu.make_async_copy(
            weight_hbm.at[pl.ds(sum(own_sizes[:part]), own_sizes[part]), :],
            weights.at[part, pl.ds(0, own_sizes[part]), :], weight_sem.at[part])

    for part in range(own_parts):
        own_copy(part).start()

    seq_count = lens.shape[0]
    held = hidden.shape[0]
    seq_len = held // seq_count
    offsets = []
    total_length = jnp.int32(0)
    for seq in range(seq_count):
        offsets.append(total_length)
        total_length = total_length + lens[seq]

    def compact_place(slot_index):
        place = jnp.full(slot_index.shape, -1, jnp.int32)
        for seq in range(seq_count):
            ahead = slot_index - seq * seq_len
            place = jnp.where((ahead >= 0) & (ahead < lens[seq]), ahead + offsets[seq], place)
        return place

    for input_copy in input_copies:
        input_copy.wait()
    place_row = compact_place(lax.broadcasted_iota(jnp.int32, (8, held), 1))[:1]
    pick = (lax.broadcasted_iota(jnp.int32, (cap, held), 0) == place_row).astype(f32).astype(jnp.bfloat16)
    live = jnp.dot(pick, hidden_here[...], preferred_element_type=f32)
    inverse_rms = lax.rsqrt(jnp.mean(live * live, axis=1, keepdims=True) + eps_norm)
    rows[0, 0:cap, :] = (live * inverse_rms * gain_here[...]).astype(jnp.bfloat16)

    place_col = compact_place(lax.broadcasted_iota(jnp.int32, (held, cap), 0))
    pick_t = (lax.broadcasted_iota(jnp.int32, (held, cap), 1) == place_col).astype(f32).astype(jnp.bfloat16)
    wide = targets_here[...]
    high = wide // 256
    digits = jnp.concatenate([high, wide - high * 256] + [jnp.zeros_like(wide)] * 14, axis=0)
    digits = digits.astype(f32).astype(jnp.bfloat16)
    tag_pair = jnp.dot(digits, pick_t, preferred_element_type=f32)
    tags[0] = (tag_pair[0:1] * 256.0 + tag_pair[1:2]).astype(jnp.int32)

    pl.semaphore_wait(barrier, len(neighbours))

    def part_rows(arrival_name):
        part, start = part_place[arrival_name]
        size = sub_rows[arrival_name[2]] if arrival_name[0] == "W" else rest_rows[arrival_name[1]]
        return weights.at[own_parts + part, pl.ds(start, size), :]

    def entry_copy(name):
        if name[0] == "W":
            sub = name[2]
            start, size = pl.multiple_of(req * quarter + sub_start[sub], 16), sub_rows[sub]
            send, recv = entry_plan[sub], weight_slot[(0, sub)]
        else:
            start, size = rest_start[name[1]], rest_rows[name[1]]
            send, recv = rest_plan[name[1]], rest_slots[name[1]]
        return pltpu.make_async_remote_copy(
            src_ref=weight_hbm.at[pl.ds(start, size), :], dst_ref=part_rows(name),
            send_sem=weight_send.at[send], recv_sem=weight_recv.at[recv],
            device_id=pair_target, device_id_type=mesh_ids)

    def weight_relay(d, sub, link):
        landing = weight_landing(d, link)
        return pltpu.make_async_remote_copy(
            src_ref=part_rows(("W", d, sub)), dst_ref=part_rows(("W", landing, sub)),
            send_sem=weight_send.at[weight_plan[((d, sub), link)]], recv_sem=weight_recv.at[weight_slot[(landing, sub)]],
            device_id=z_target(1 if link == "up" else 3), device_id_type=mesh_ids)

    def row_index(group):
        return all_groups.index(group)

    def piece_copy(group, piece, link):
        landing = row_index(row_landing(*group, link))
        start = piece * piece_rows
        there = start + (cap if link == "partner" else 0)
        recv = (partner_recv if link == "partner" else row_recv).at[landing * pieces + piece]
        return pltpu.make_async_remote_copy(
            src_ref=rows.at[row_index(group), pl.ds(start, piece_rows), :],
            dst_ref=rows.at[landing, pl.ds(there, piece_rows), :],
            send_sem=row_send.at[row_plan[(group, piece, link)]], recv_sem=recv,
            device_id=row_target(link), device_id_type=mesh_ids)

    def tag_copy(group, link):
        landing = row_index(row_landing(*group, link)) * 2 + (1 if link == "partner" else 0)
        return pltpu.make_async_remote_copy(
            src_ref=tags.at[row_index(group) * 2], dst_ref=tags.at[landing],
            send_sem=tag_send.at[tag_plan[(group, link)]], recv_sem=tag_recv.at[landing],
            device_id=row_target(link), device_id_type=mesh_ids)

    def tag_here(landing):
        return pltpu.make_async_copy(tags.at[landing], tags.at[landing], tag_recv.at[landing])

    def send_onward(p, dy, piece):
        taken = row_links(p, dy, piece) + ["partner"]
        for link in taken:
            piece_copy((p, dy), piece, link).start()
        if piece == 0:
            for link in taken:
                tag_copy((p, dy), link).start()

    entry_copy(entries[0]).start()
    for piece in (0, 2, 1, 3):
        send_onward(0, 0, piece)
    for name in entries[1:]:
        entry_copy(name).start()

    def arrival(event):
        if event[0] == "D":
            here = part_rows(event)
            pltpu.make_async_copy(here, here, weight_recv.at[rest_slots[event[1]]]).wait()
        elif event[0] == "W":
            here = part_rows(event)
            pltpu.make_async_copy(here, here, weight_recv.at[weight_slot[event[1:]]]).wait()
            for link in weight_links(*event[1:]):
                weight_relay(event[1], event[2], link).start()
        else:
            group, piece = event[1:3], event[3]
            here = rows.at[row_index(group), pl.ds(piece * piece_rows, piece_rows), :]
            pltpu.make_async_copy(here, here, row_recv.at[row_index(group) * pieces + piece]).wait()
            if piece == 0:
                tag_here(row_index(group) * 2).wait()
            send_onward(*group, piece)

    my_place = (chip_y * 2 + side_x) * 2 + core

    def stat_copy(slot, group, other):
        return pltpu.make_async_remote_copy(
            src_ref=running.at[slot, other], dst_ref=stats_in.at[my_place],
            send_sem=stat_send.at[slot * 2 + other], recv_sem=stat_recv,
            device_id=(req, group_owner(group, other)), device_id_type=mesh_ids)

    own_first = me * columns
    pair_first = vocab_id(pair_x, chip_y, core) * columns

    def part_blocks(part):
        if part < own_parts:
            return [(0, own_sizes[part], own_first + sum(own_sizes[:part]))]
        blocks = []
        for name in parts[part - own_parts]:
            start = part_place[name][1]
            if name[0] == "W":
                first = lax.rem(req + name[1], side) * quarter + sub_start[name[2]]
                blocks.append((start, sub_rows[name[2]], pair_first + first))
            else:
                blocks.append((start, rest_rows[name[1]], pair_first + rest_start[name[1]]))
        return blocks

    for part in range(part_count):
        filled = 0
        for start, size, first in part_blocks(part):
            column_ids[part, pl.ds(start, size), :] = lax.broadcasted_iota(jnp.int32, (size, cap), 0) + first
            filled += size
        if filled < part_height:
            missing = part_height - filled
            column_ids[part, pl.ds(filled, missing), :] = jnp.full((missing, cap), -1, jnp.int32)
            weights[part, pl.ds(filled, missing), :] = jnp.zeros((missing, depth), jnp.bfloat16)
    empty = jnp.where(lax.rem(lax.broadcasted_iota(jnp.int32, (8, cap), 0), 4) == 0, -1e30, 0.0)
    for group in range(group_count):
        for other in range(2):
            running[group, other] = empty

    sure = part_height - ragged

    def tile(first_group, count, part):
        if count == 1:
            taken = rows[first_group]
        else:
            taken = rows[pl.ds(first_group, count)].reshape(count * 2 * cap, depth)
        logits = lax.dot_general(weights[part], taken, (((1,), (1,)), ((), ())), preferred_element_type=f32)
        for block_index in range(2 * count):
            group = first_group + block_index // 2
            other = block_index % 2
            lanes = slice(block_index * cap, (block_index + 1) * cap)
            tag = tags[group * 2 + other]
            ids_tail = column_ids[part, sure:, :]
            main = logits[:sure, lanes]
            tail = jnp.where(ids_tail >= 0, logits[sure:, lanes], -1e30)
            peak = jnp.maximum(jnp.max(main, axis=0, keepdims=True), jnp.max(tail, axis=0, keepdims=True))
            shifted = main - peak
            exponent = jnp.exp(shifted)
            shifted_tail = tail - peak
            exponent_tail = jnp.exp(shifted_tail)
            chosen = jnp.where(column_ids[part, :sure, :] == tag, main, 0.0)
            chosen_tail = jnp.where(ids_tail == tag, tail, 0.0)

            def summed(many, few):
                return jnp.sum(many, axis=0, keepdims=True) + jnp.sum(few, axis=0, keepdims=True)

            total = summed(exponent, exponent_tail)
            spread = summed(exponent * shifted, exponent_tail * shifted_tail)
            picked = summed(chosen, chosen_tail)
            before = running[group, other]
            joint = jnp.maximum(before[0:1], peak)
            drop_before = before[0:1] - joint
            drop = peak - joint
            factor_before = jnp.exp(drop_before)
            factor = jnp.exp(drop)
            spread = factor_before * (before[2:3] + drop_before * before[1:2]) + factor * (spread + drop * total)
            total = factor_before * before[1:2] + factor * total
            running[group, other] = jnp.concatenate([joint, total, spread, picked + before[3:4]] * 2, axis=0)

    def at_step(step, index):
        for event in steps[index][0]:
            arrival(event)
        if index == last_own_step + 1:
            pl.semaphore_signal(token_x, inc=1, device_id=pair_target, device_id_type=mesh_ids)
        if index == len(steps) - 3:
            pl.semaphore_wait(token_x, 1)
            for ahead in range(1, side):
                pl.semaphore_signal(token_z, inc=1, device_id=z_target(ahead), device_id_type=mesh_ids)

    busy_steps = [index for index in range(len(steps))
                  if steps[index][0] or index in (last_own_step + 1, len(steps) - 3)]

    def dispatch(step, low, high):
        inside = [index for index in busy_steps if low <= index < high]
        if not inside:
            return
        if len(inside) == 1:
            @pl.when(step == inside[0])
            def _():
                at_step(step, inside[0])
            return
        middle = inside[len(inside) // 2]

        @pl.when(step < middle)
        def _():
            dispatch(step, low, middle)

        @pl.when(step >= middle)
        def _():
            dispatch(step, middle, high)

    def one_step(step, carry):
        dispatch(step, 0, len(steps))
        code = jnp.int32(0)
        for index, (events, part, pair) in enumerate(steps):
            code = jnp.where(step == index, part * 8 + pair, code)
        part_now = code // 8
        pair_now = lax.rem(code, 8)
        first_now = jnp.where(pair_now < side, pair_now * 2, pair_now - side)

        def partner_here(group):
            for piece in range(pieces):
                there = rows.at[group, pl.ds(cap + piece * piece_rows, piece_rows), :]
                pltpu.make_async_copy(there, there, partner_recv.at[group * pieces + piece]).wait()
            tag_here(group * 2 + 1).wait()

        @pl.when(part_now == 0)
        def _():
            partner_here(first_now)

            @pl.when(pair_now < side)
            def _():
                partner_here(first_now + 1)

        @pl.when(pair_now < side)
        def _():
            tile(first_now, 2, part_now)

        @pl.when(pair_now >= side)
        def _():
            tile(first_now, 1, part_now)

        @pl.when(part_now == part_count - 1)
        def _():
            for member in range(2):
                slot = pair_now * 2 + member
                p = jnp.int32(0)
                dy = jnp.int32(0)
                for index in range(member, group_count, 2):
                    p = jnp.where(slot == index, all_groups[index][0], p)
                    dy = jnp.where(slot == index, all_groups[index][1], dy)
                stat_copy(slot, (p, dy), 1).start()
                if member == 1:
                    stat_copy(slot, (p, dy), 0).start()
                else:
                    @pl.when(pair_now == 0)
                    def _():
                        stats_in[my_place] = running[0, 0]

                    @pl.when(pair_now > 0)
                    def _():
                        stat_copy(slot, (p, dy), 0).start()
        return carry

    for part in range(own_parts):
        own_copy(part).wait()
    lax.fori_loop(0, len(steps), one_step, 0)

    sources = 2 * group_count
    pltpu.make_async_copy(stats_in.at[pl.ds(0, sources - 1)], stats_in.at[pl.ds(0, sources - 1)], stat_recv).wait()

    peak = stats_in[0]
    for index in range(1, sources):
        peak = jnp.maximum(peak, stats_in[index])
    peak = peak[0:1]
    row_total = jnp.zeros((1, cap), f32)
    spread = jnp.zeros((1, cap), f32)
    picked = jnp.zeros((1, cap), f32)
    for index in range(sources):
        stat = stats_in[index]
        below = stat[0:1] - peak
        factor = jnp.exp(below)
        row_total = row_total + stat[1:2] * factor
        spread = spread + factor * (stat[2:3] + below * stat[1:2])
        picked = picked + stat[3:4]
    log_total = jnp.log(row_total)
    logprob = jnp.broadcast_to(picked - peak - log_total, (seq_count, cap))
    entropy = jnp.broadcast_to(log_total - spread / row_total, (seq_count, cap))

    request = lax.broadcasted_iota(jnp.int32, (seq_count, cap), 0)
    lane = lax.broadcasted_iota(jnp.int32, (seq_count, cap), 1)
    offset = jnp.zeros((seq_count, cap), jnp.int32)
    length = jnp.zeros((seq_count, cap), jnp.int32)
    for seq in range(seq_count):
        offset = jnp.where(request == seq, offsets[seq], offset)
        length = jnp.where(request == seq, lens[seq], length)
    bit = 1
    while bit < cap:
        moved = (offset & bit) != 0
        logprob = jnp.where(moved, pltpu.roll(logprob, cap - bit, 1), logprob)
        entropy = jnp.where(moved, pltpu.roll(entropy, cap - bit, 1), entropy)
        bit *= 2
    logprob = jnp.where(lane < length, logprob, 0.0)
    entropy = jnp.where(lane < length, entropy, 0.0)
    both = logprob + pltpu.roll(entropy, seq_len, 1)
    half = seq_count // 2
    mine = req * members + me
    fin[mine] = both[:half] + pltpu.roll(both[half:], cap // 2, 1)

    pl.semaphore_wait(token_z, side - 1)

    def fin_copy(step):
        other = lax.rem(mine + step, members * side)
        return pltpu.make_async_remote_copy(
            src_ref=fin.at[mine], dst_ref=fin.at[mine], send_sem=fin_send, recv_sem=fin_recv,
            device_id=(other // members, lax.rem(other, members)), device_id_type=mesh_ids)

    def send_fin(step, carry):
        fin_copy(step).start()
        return carry

    lax.fori_loop(1, members * side, send_fin, 0)
    others = fin.at[pl.ds(0, members * side - 1)]
    pltpu.make_async_copy(others, others, fin_recv).wait()

    for seq in range(seq_count):
        wanted = slots[seq]
        owner = lax.div(wanted, seq_count)
        inside = lax.rem(wanted, seq_count)
        found = fin[owner]
        turned = pltpu.roll(found, cap // 2, 1)
        found = jnp.where(inside >= half, turned, found)
        level = lax.rem(inside, half)
        row = lax.broadcasted_iota(jnp.int32, (half, cap), 0)
        gathered[pl.ds(seq, 1), :] = jnp.sum(jnp.where(row == level, found, 0.0), axis=0, keepdims=True)
    out[0] = gathered[:, 0:seq_len]
    out[1] = gathered[:, seq_len:2 * seq_len]

    def drain(index, carry):
        here = rows.at[0, pl.ds(0, piece_rows), :]
        pltpu.make_async_copy(here, here, row_send.at[index]).wait()
        return carry

    lax.fori_loop(0, len(row_plan), drain, 0)
    for (d, sub), link in weight_plan:
        weight_relay(d, sub, link).wait_send()
    for name in entries:
        entry_copy(name).wait_send()

    def drain_tags(index, carry):
        pltpu.make_async_copy(tags.at[0], tags.at[0], tag_send.at[index]).wait()
        return carry

    lax.fori_loop(0, len(tag_plan), drain_tags, 0)

    def drain_stats(index, carry):
        pltpu.make_async_copy(stats_in.at[0], stats_in.at[0], stat_send.at[index]).wait()
        return carry

    lax.fori_loop(1, sources, drain_stats, 0)
    pltpu.make_async_copy(others, others, fin_send).wait()


def local(hidden_states, norm_gain, head_weight, targets, lengths, slot_of):
    held, depth = hidden_states.shape
    seq_count = lengths.shape[0]
    seq_len = held // seq_count
    columns = head_weight.shape[1]
    members = 2 * side * side
    vmem = pl.BlockSpec(memory_space=pltpu.VMEM)
    smem = pl.BlockSpec(memory_space=pltpu.SMEM)
    dma = pltpu.SemaphoreType.DMA
    regular = pltpu.SemaphoreType.REGULAR
    out = jax.ShapeDtypeStruct((2, seq_count, seq_len), f32)
    both = pl.pallas_call(
        kernel,
        out_shape=out,
        in_specs=[smem, smem] + [pl.BlockSpec(memory_space=pl.ANY)] * 4,
        out_specs=vmem,
        scratch_shapes=[
            pltpu.VMEM((held, depth), jnp.bfloat16),
            pltpu.VMEM((1, depth), f32),
            pltpu.VMEM((1, held), jnp.int32),
            dma((3,)),
            pltpu.VMEM((part_count, part_height, depth), jnp.bfloat16),
            pltpu.VMEM((part_count, part_height, cap), jnp.int32),
            pltpu.VMEM((group_count, 2 * cap, depth), jnp.bfloat16),
            pltpu.VMEM((2 * group_count, 1, cap), jnp.int32),
            pltpu.VMEM((group_count, 2, 8, cap), f32),
            pltpu.VMEM((2 * group_count, 8, cap), f32),
            pltpu.VMEM((members * side, seq_count // 2, cap), f32),
            pltpu.VMEM((seq_count, cap), f32),
            dma((own_parts,)),
            dma((len(row_plan),)),
            dma((group_count * pieces,)),
            dma((group_count * pieces,)),
            dma((weight_sends,)),
            dma((rest_slots[-1] + 1,)),
            dma((len(tag_plan),)),
            dma((2 * group_count,)),
            dma((2 * group_count,)),
            dma,
            regular,
            regular,
            dma,
            dma,
        ],
        compiler_params=pltpu.CompilerParams(collective_id=0, has_side_effects=True, vmem_limit_bytes=60 << 20),
        name="head_stats",
    )(lengths, slot_of, hidden_states, norm_gain.reshape(1, depth), targets.reshape(1, held), head_weight.T)
    return (both[0], both[1])


def solution(mesh):
    rows = jax.sharding.PartitionSpec(("req", "vocab"), None)
    flat = jax.sharding.PartitionSpec(("req", "vocab"))
    in_specs = (rows, jax.sharding.PartitionSpec(), jax.sharding.PartitionSpec(None, "vocab"), flat, flat, flat)
    return jax.shard_map(local, mesh=mesh, in_specs=in_specs, out_specs=(rows, rows), check_vma=False)
```

```python
import jax
import jax.numpy as jnp
from jax import lax
from jax.experimental import pallas as pl
from jax.experimental.pallas import tpu as pltpu

eps_norm = 1e-05
side = 4
cap = 128
pieces = 4
piece_rows = cap // pieces
group_count = 2 * side
mesh_ids = pl.DeviceIdType.MESH
f32 = jnp.float32

own_part_sizes = (504, 496)
sub_rows = (32, 32, 16, 32, 64, 32)
rest_rows = (80, 88)
entries = [("W", 0, 0), ("W", 0, 1), ("W", 0, 2), ("W", 0, 3), ("W", 0, 4), ("W", 0, 5), ("D", 0), ("D", 1)]
parts = [[("W", 0, 0), ("W", 0, 1), ("W", 0, 2), ("W", 3, 0), ("W", 1, 0), ("W", 0, 3), ("W", 3, 1), ("W", 1, 1), ("W", 3, 2), ("W", 1, 2), ("W", 2, 0), ("W", 1, 3), ("W", 0, 4), ("W", 3, 3), ("W", 2, 1), ("W", 0, 5)], [("W", 2, 2), ("W", 2, 3), ("W", 3, 4), ("D", 0), ("W", 1, 4), ("W", 3, 5), ("W", 1, 5), ("W", 2, 4), ("W", 2, 5), ("D", 1)]]
steps = [
    ([], 0, 4),
    ([], 1, 4),
    ([("W", 0, 0), ("R", 1, 0, 0), ("R", 0, 3, 0), ("R", 0, 1, 0), ("W", 0, 1), ("R", 0, 3, 2), ("R", 0, 1, 2), ("R", 1, 0, 2), ("W", 0, 2), ("W", 3, 0), ("W", 1, 0), ("R", 1, 0, 1), ("R", 0, 3, 1), ("R", 0, 1, 1), ("W", 0, 3), ("W", 3, 1), ("W", 1, 1), ("R", 0, 3, 3), ("R", 0, 1, 3), ("R", 1, 0, 3), ("W", 3, 2), ("W", 1, 2)], 0, 5),
    ([], 0, 1),
    ([("R", 1, 3, 0), ("R", 1, 1, 0), ("R", 1, 3, 2), ("W", 2, 0), ("W", 1, 3)], 1, 5),
    ([("W", 0, 4)], 1, 1),
    ([("R", 0, 2, 0), ("R", 1, 1, 2), ("R", 1, 1, 1), ("W", 3, 3), ("W", 2, 1), ("W", 0, 5)], 2, 0),
    ([("W", 2, 2), ("R", 0, 2, 2), ("R", 0, 2, 1), ("R", 1, 3, 3)], 2, 1),
    ([("W", 2, 3), ("R", 1, 3, 1), ("R", 1, 1, 3), ("R", 0, 2, 3)], 0, 2),
    ([("W", 3, 4), ("D", 0), ("R", 1, 2, 0), ("R", 1, 2, 1), ("R", 1, 2, 2)], 1, 2),
    ([("W", 1, 4), ("W", 3, 5)], 2, 2),
    ([("R", 1, 2, 3), ("W", 1, 5)], 0, 3),
    ([], 1, 3),
    ([("W", 2, 4)], 2, 3),
    ([("W", 2, 5), ("D", 1)], 3, 3),
    ([], 3, 2),
    ([], 3, 1),
    ([], 3, 5),
    ([], 3, 4),
]
sub_start = [sum(sub_rows[:index]) for index in range(len(sub_rows))]
quarter = sum(sub_rows)
part_place = {}
part_sizes = []
for part_index, part_list in enumerate(parts):
    filled = 0
    for part_piece in part_list:
        part_place[part_piece] = (part_index, filled)
        filled += sub_rows[part_piece[2]] if part_piece[0] == "W" else rest_rows[part_piece[1]]
    part_sizes.append(filled)
rest_start = [side * quarter + sum(rest_rows[:index]) for index in range(len(rest_rows))]


def row_links(p, dy, q):
    taken = []
    x_first = q < 2
    upward = q % 2 == 0
    if x_first:
        if (p, dy) == (0, 0):
            taken.append("x")
        if dy == 0:
            taken += ["up", "down"]
    else:
        if (p, dy) == (0, 0):
            taken += ["up", "down"]
        if p == 0:
            taken.append("x")
    if x_first or p == 0:
        if dy == 3 and upward:
            taken.append("up")
        if dy == 1 and not upward:
            taken.append("down")
    return taken


def row_landing(p, dy, link):
    if link == "x":
        return (1 - p, dy)
    if link == "partner":
        return (p, dy)
    return (p, (dy + (3 if link == "up" else 1)) % side)


def weight_links(d, sub):
    if d == 0:
        return ["up", "down"]
    if d == 3 and sub % 2 == 0:
        return ["up"]
    if d == 1 and sub % 2 == 1:
        return ["down"]
    return []


def weight_landing(d, link):
    return (d + (3 if link == "up" else 1)) % side


all_groups = [(0, 0), (0, 1), (0, 3), (1, 0), (1, 1), (1, 3), (0, 2), (1, 2)]
row_plan = {}
tag_plan = {}
tag_first = {}
for plan_group in all_groups:
    for plan_link in ["partner", "x", "up", "down"]:
        for plan_piece in range(pieces):
            if plan_link == "partner" or plan_link in row_links(*plan_group, plan_piece):
                row_plan[(plan_group, plan_piece, plan_link)] = len(row_plan)
                landing_group = row_landing(*plan_group, plan_link)
                if plan_piece == 0:
                    tag_plan[(plan_group, plan_link)] = len(tag_plan)
weight_arrivals = [(d, sub) for d in range(side) for sub in range(len(sub_rows))]
weight_slot = {arrival: index for index, arrival in enumerate(weight_arrivals)}
rest_slots = [len(weight_arrivals) + index for index in range(len(rest_rows))]
weight_plan = {}
for plan_arrival in weight_arrivals:
    for plan_link in weight_links(*plan_arrival):
        weight_plan[(plan_arrival, plan_link)] = len(weight_plan)
entry_plan = {sub: len(weight_plan) + sub for sub in range(len(sub_rows))}
rest_plan = [len(weight_plan) + len(sub_rows) + index for index in range(len(rest_rows))]
weight_sends = rest_plan[-1] + 1
own_sizes = own_part_sizes
own_parts = len(own_sizes)
part_count = own_parts + len(parts)
part_height = max(own_sizes + tuple(part_sizes))
ragged = part_height - min(own_sizes + tuple(part_sizes))
last_own_step = max(index for index, step_entry in enumerate(steps) if step_entry[1] == 0)


def kernel(lens, slots, hidden, gain, targets, weight_hbm, out, *scratch):
    (hidden_here, gain_here, targets_here, input_sem, weights, column_ids, rows, tags, running, stats_in, fin, gathered, weight_sem, row_send, row_recv, partner_recv, weight_send, weight_recv, tag_send, tag_recv,
     stat_send, stat_recv, token_x, token_z, fin_send, fin_recv) = scratch
    input_copies = [pltpu.make_async_copy(source, target, input_sem.at[index]) for index, (source, target) in enumerate(
        [(hidden, hidden_here), (gain, gain_here), (targets, targets_here)])]
    for input_copy in input_copies:
        input_copy.start()
    req = lax.axis_index("req")
    me = lax.axis_index("vocab")
    core = lax.rem(me, 2)
    chip_x = lax.rem(me // 2, side)
    chip_y = me // (2 * side)
    members = 2 * side * side
    columns, depth = weight_hbm.shape
    side_x = lax.rem(chip_x, 2)
    pair_x = side - 1 - chip_x

    def vocab_id(x, y, the_core):
        return (y * side + x) * 2 + the_core

    def group_owner(group, other):
        p, dy = group
        x = chip_x + p * (1 - 2 * side_x)
        return vocab_id(x, lax.rem(chip_y + dy, side), (1 - core) if other else core)

    def row_target(link):
        if link == "partner":
            return (req, vocab_id(chip_x, chip_y, 1 - core))
        if link == "x":
            return (req, group_owner((1, 0), False))
        return (req, group_owner((0, 1 if link == "up" else 3), False))

    def z_target(ahead):
        return (lax.rem(req + ahead, side), me)

    pair_target = (req, vocab_id(pair_x, chip_y, core))

    barrier = pltpu.get_barrier_semaphore()
    neighbours = [row_target(link) for link in ("partner", "x", "up", "down")] + [pair_target, z_target(1), z_target(3)]
    for neighbour in neighbours:
        pl.semaphore_signal(barrier, inc=1, device_id=neighbour, device_id_type=mesh_ids)

    def own_copy(part):
        return pltpu.make_async_copy(
            weight_hbm.at[pl.ds(sum(own_sizes[:part]), own_sizes[part]), :],
            weights.at[part, pl.ds(0, own_sizes[part]), :], weight_sem.at[part])

    for part in range(own_parts):
        own_copy(part).start()

    seq_count = lens.shape[0]
    held = hidden.shape[0]
    seq_len = held // seq_count
    offsets = []
    total_length = jnp.int32(0)
    for seq in range(seq_count):
        offsets.append(total_length)
        total_length = total_length + lens[seq]

    def compact_place(slot_index):
        place = jnp.full(slot_index.shape, -1, jnp.int32)
        for seq in range(seq_count):
            ahead = slot_index - seq * seq_len
            place = jnp.where((ahead >= 0) & (ahead < lens[seq]), ahead + offsets[seq], place)
        return place

    for input_copy in input_copies:
        input_copy.wait()
    place_row = compact_place(lax.broadcasted_iota(jnp.int32, (8, held), 1))[:1]
    pick = (lax.broadcasted_iota(jnp.int32, (cap, held), 0) == place_row).astype(f32).astype(jnp.bfloat16)
    live = jnp.dot(pick, hidden_here[...], preferred_element_type=f32)
    inverse_rms = lax.rsqrt(jnp.mean(live * live, axis=1, keepdims=True) + eps_norm)
    rows[0, 0:cap, :] = (live * inverse_rms * gain_here[...]).astype(jnp.bfloat16)

    place_col = compact_place(lax.broadcasted_iota(jnp.int32, (held, cap), 0))
    pick_t = (lax.broadcasted_iota(jnp.int32, (held, cap), 1) == place_col).astype(f32).astype(jnp.bfloat16)
    wide = targets_here[...]
    high = wide // 256
    digits = jnp.concatenate([high, wide - high * 256] + [jnp.zeros_like(wide)] * 14, axis=0)
    digits = digits.astype(f32).astype(jnp.bfloat16)
    tag_pair = jnp.dot(digits, pick_t, preferred_element_type=f32)
    tags[0] = (tag_pair[0:1] * 256.0 + tag_pair[1:2]).astype(jnp.int32)

    pl.semaphore_wait(barrier, len(neighbours))

    def part_rows(arrival_name):
        part, start = part_place[arrival_name]
        size = sub_rows[arrival_name[2]] if arrival_name[0] == "W" else rest_rows[arrival_name[1]]
        return weights.at[own_parts + part, pl.ds(start, size), :]

    def entry_copy(name):
        if name[0] == "W":
            sub = name[2]
            start, size = pl.multiple_of(req * quarter + sub_start[sub], 16), sub_rows[sub]
            send, recv = entry_plan[sub], weight_slot[(0, sub)]
        else:
            start, size = rest_start[name[1]], rest_rows[name[1]]
            send, recv = rest_plan[name[1]], rest_slots[name[1]]
        return pltpu.make_async_remote_copy(
            src_ref=weight_hbm.at[pl.ds(start, size), :], dst_ref=part_rows(name),
            send_sem=weight_send.at[send], recv_sem=weight_recv.at[recv],
            device_id=pair_target, device_id_type=mesh_ids)

    def weight_relay(d, sub, link):
        landing = weight_landing(d, link)
        return pltpu.make_async_remote_copy(
            src_ref=part_rows(("W", d, sub)), dst_ref=part_rows(("W", landing, sub)),
            send_sem=weight_send.at[weight_plan[((d, sub), link)]], recv_sem=weight_recv.at[weight_slot[(landing, sub)]],
            device_id=z_target(1 if link == "up" else 3), device_id_type=mesh_ids)

    def row_index(group):
        return all_groups.index(group)

    def piece_copy(group, piece, link):
        landing = row_index(row_landing(*group, link))
        start = piece * piece_rows
        there = start + (cap if link == "partner" else 0)
        recv = (partner_recv if link == "partner" else row_recv).at[landing * pieces + piece]
        return pltpu.make_async_remote_copy(
            src_ref=rows.at[row_index(group), pl.ds(start, piece_rows), :],
            dst_ref=rows.at[landing, pl.ds(there, piece_rows), :],
            send_sem=row_send.at[row_plan[(group, piece, link)]], recv_sem=recv,
            device_id=row_target(link), device_id_type=mesh_ids)

    def tag_copy(group, link):
        landing = row_index(row_landing(*group, link)) * 2 + (1 if link == "partner" else 0)
        return pltpu.make_async_remote_copy(
            src_ref=tags.at[row_index(group) * 2], dst_ref=tags.at[landing],
            send_sem=tag_send.at[tag_plan[(group, link)]], recv_sem=tag_recv.at[landing],
            device_id=row_target(link), device_id_type=mesh_ids)

    def tag_here(landing):
        return pltpu.make_async_copy(tags.at[landing], tags.at[landing], tag_recv.at[landing])

    def send_onward(p, dy, piece):
        taken = row_links(p, dy, piece) + ["partner"]
        for link in taken:
            piece_copy((p, dy), piece, link).start()
        if piece == 0:
            for link in taken:
                tag_copy((p, dy), link).start()

    entry_copy(entries[0]).start()
    for piece in (0, 2, 1, 3):
        send_onward(0, 0, piece)
    for name in entries[1:]:
        entry_copy(name).start()

    def arrival(event):
        if event[0] == "D":
            here = part_rows(event)
            pltpu.make_async_copy(here, here, weight_recv.at[rest_slots[event[1]]]).wait()
        elif event[0] == "W":
            here = part_rows(event)
            pltpu.make_async_copy(here, here, weight_recv.at[weight_slot[event[1:]]]).wait()
            for link in weight_links(*event[1:]):
                weight_relay(event[1], event[2], link).start()
        else:
            group, piece = event[1:3], event[3]
            here = rows.at[row_index(group), pl.ds(piece * piece_rows, piece_rows), :]
            pltpu.make_async_copy(here, here, row_recv.at[row_index(group) * pieces + piece]).wait()
            if piece == 0:
                tag_here(row_index(group) * 2).wait()
            send_onward(*group, piece)

    my_place = (chip_y * 2 + side_x) * 2 + core

    def stat_copy(slot, group, other):
        return pltpu.make_async_remote_copy(
            src_ref=running.at[slot, other], dst_ref=stats_in.at[my_place],
            send_sem=stat_send.at[slot * 2 + other], recv_sem=stat_recv,
            device_id=(req, group_owner(group, other)), device_id_type=mesh_ids)

    own_first = me * columns
    pair_first = vocab_id(pair_x, chip_y, core) * columns

    def part_blocks(part):
        if part < own_parts:
            return [(0, own_sizes[part], own_first + sum(own_sizes[:part]))]
        blocks = []
        for name in parts[part - own_parts]:
            start = part_place[name][1]
            if name[0] == "W":
                first = lax.rem(req + name[1], side) * quarter + sub_start[name[2]]
                blocks.append((start, sub_rows[name[2]], pair_first + first))
            else:
                blocks.append((start, rest_rows[name[1]], pair_first + rest_start[name[1]]))
        return blocks

    for part in range(part_count):
        filled = 0
        for start, size, first in part_blocks(part):
            column_ids[part, pl.ds(start, size), :] = lax.broadcasted_iota(jnp.int32, (size, cap), 0) + first
            filled += size
        if filled < part_height:
            missing = part_height - filled
            column_ids[part, pl.ds(filled, missing), :] = jnp.full((missing, cap), -1, jnp.int32)
            weights[part, pl.ds(filled, missing), :] = jnp.zeros((missing, depth), jnp.bfloat16)
    empty = jnp.where(lax.rem(lax.broadcasted_iota(jnp.int32, (8, cap), 0), 4) == 0, -1e30, 0.0)
    for group in range(group_count):
        for other in range(2):
            running[group, other] = empty

    sure = part_height - ragged

    def tile(first_group, count, part):
        if count == 1:
            taken = rows[first_group]
        else:
            taken = rows[pl.ds(first_group, count)].reshape(count * 2 * cap, depth)
        logits = lax.dot_general(weights[part], taken, (((1,), (1,)), ((), ())), preferred_element_type=f32)
        for block_index in range(2 * count):
            group = first_group + block_index // 2
            other = block_index % 2
            lanes = slice(block_index * cap, (block_index + 1) * cap)
            tag = tags[group * 2 + other]
            ids_tail = column_ids[part, sure:, :]
            main = logits[:sure, lanes]
            tail = jnp.where(ids_tail >= 0, logits[sure:, lanes], -1e30)
            peak = jnp.maximum(jnp.max(main, axis=0, keepdims=True), jnp.max(tail, axis=0, keepdims=True))
            shifted = main - peak
            exponent = jnp.exp(shifted)
            shifted_tail = tail - peak
            exponent_tail = jnp.exp(shifted_tail)
            chosen = jnp.where(column_ids[part, :sure, :] == tag, main, 0.0)
            chosen_tail = jnp.where(ids_tail == tag, tail, 0.0)

            def summed(many, few):
                return jnp.sum(many, axis=0, keepdims=True) + jnp.sum(few, axis=0, keepdims=True)

            total = summed(exponent, exponent_tail)
            spread = summed(exponent * shifted, exponent_tail * shifted_tail)
            picked = summed(chosen, chosen_tail)
            before = running[group, other]
            joint = jnp.maximum(before[0:1], peak)
            drop_before = before[0:1] - joint
            drop = peak - joint
            factor_before = jnp.exp(drop_before)
            factor = jnp.exp(drop)
            spread = factor_before * (before[2:3] + drop_before * before[1:2]) + factor * (spread + drop * total)
            total = factor_before * before[1:2] + factor * total
            running[group, other] = jnp.concatenate([joint, total, spread, picked + before[3:4]] * 2, axis=0)

    def at_step(step, index):
        for event in steps[index][0]:
            arrival(event)
        if index == last_own_step + 1:
            pl.semaphore_signal(token_x, inc=1, device_id=pair_target, device_id_type=mesh_ids)
        if index == len(steps) - 3:
            pl.semaphore_wait(token_x, 1)
            for ahead in range(1, side):
                pl.semaphore_signal(token_z, inc=1, device_id=z_target(ahead), device_id_type=mesh_ids)

    busy_steps = [index for index in range(len(steps))
                  if steps[index][0] or index in (last_own_step + 1, len(steps) - 3)]

    def dispatch(step, low, high):
        inside = [index for index in busy_steps if low <= index < high]
        if not inside:
            return
        if len(inside) == 1:
            @pl.when(step == inside[0])
            def _():
                at_step(step, inside[0])
            return
        middle = inside[len(inside) // 2]

        @pl.when(step < middle)
        def _():
            dispatch(step, low, middle)

        @pl.when(step >= middle)
        def _():
            dispatch(step, middle, high)

    def one_step(step, carry):
        dispatch(step, 0, len(steps))
        code = jnp.int32(0)
        for index, (events, part, pair) in enumerate(steps):
            code = jnp.where(step == index, part * 8 + pair, code)
        part_now = code // 8
        pair_now = lax.rem(code, 8)
        first_now = jnp.where(pair_now < side, pair_now * 2, pair_now - side)

        def partner_here(group):
            for piece in range(pieces):
                there = rows.at[group, pl.ds(cap + piece * piece_rows, piece_rows), :]
                pltpu.make_async_copy(there, there, partner_recv.at[group * pieces + piece]).wait()
            tag_here(group * 2 + 1).wait()

        @pl.when(part_now == 0)
        def _():
            partner_here(first_now)

            @pl.when(pair_now < side)
            def _():
                partner_here(first_now + 1)

        @pl.when(pair_now < side)
        def _():
            tile(first_now, 2, part_now)

        @pl.when(pair_now >= side)
        def _():
            tile(first_now, 1, part_now)

        @pl.when(part_now == part_count - 1)
        def _():
            def send_stats(slot, may_be_own):
                p = jnp.int32(0)
                dy = jnp.int32(0)
                for index in range(group_count):
                    p = jnp.where(slot == index, all_groups[index][0], p)
                    dy = jnp.where(slot == index, all_groups[index][1], dy)
                stat_copy(slot, (p, dy), 1).start()
                if not may_be_own:
                    stat_copy(slot, (p, dy), 0).start()
                    return

                @pl.when(slot == 0)
                def _():
                    stats_in[my_place] = running[0, 0]

                @pl.when(slot > 0)
                def _():
                    stat_copy(slot, (p, dy), 0).start()

            send_stats(first_now, True)

            @pl.when(pair_now < side)
            def _():
                send_stats(first_now + 1, False)

        return carry

    for part in range(own_parts):
        own_copy(part).wait()
    lax.fori_loop(0, len(steps), one_step, 0)

    sources = 2 * group_count
    pltpu.make_async_copy(stats_in.at[pl.ds(0, sources - 1)], stats_in.at[pl.ds(0, sources - 1)], stat_recv).wait()

    peak = stats_in[0]
    for index in range(1, sources):
        peak = jnp.maximum(peak, stats_in[index])
    peak = peak[0:1]
    row_total = jnp.zeros((1, cap), f32)
    spread = jnp.zeros((1, cap), f32)
    picked = jnp.zeros((1, cap), f32)
    for index in range(sources):
        stat = stats_in[index]
        below = stat[0:1] - peak
        factor = jnp.exp(below)
        row_total = row_total + stat[1:2] * factor
        spread = spread + factor * (stat[2:3] + below * stat[1:2])
        picked = picked + stat[3:4]
    log_total = jnp.log(row_total)
    logprob = jnp.broadcast_to(picked - peak - log_total, (seq_count, cap))
    entropy = jnp.broadcast_to(log_total - spread / row_total, (seq_count, cap))

    request = lax.broadcasted_iota(jnp.int32, (seq_count, cap), 0)
    lane = lax.broadcasted_iota(jnp.int32, (seq_count, cap), 1)
    offset = jnp.zeros((seq_count, cap), jnp.int32)
    length = jnp.zeros((seq_count, cap), jnp.int32)
    for seq in range(seq_count):
        offset = jnp.where(request == seq, offsets[seq], offset)
        length = jnp.where(request == seq, lens[seq], length)
    bit = 1
    while bit < cap:
        moved = (offset & bit) != 0
        logprob = jnp.where(moved, pltpu.roll(logprob, cap - bit, 1), logprob)
        entropy = jnp.where(moved, pltpu.roll(entropy, cap - bit, 1), entropy)
        bit *= 2
    logprob = jnp.where(lane < length, logprob, 0.0)
    entropy = jnp.where(lane < length, entropy, 0.0)
    both = logprob + pltpu.roll(entropy, seq_len, 1)
    half = seq_count // 2
    mine = req * members + me
    fin[mine] = both[:half] + pltpu.roll(both[half:], cap // 2, 1)

    pl.semaphore_wait(token_z, side - 1)

    def fin_copy(step):
        other = lax.rem(mine + step, members * side)
        return pltpu.make_async_remote_copy(
            src_ref=fin.at[mine], dst_ref=fin.at[mine], send_sem=fin_send, recv_sem=fin_recv,
            device_id=(other // members, lax.rem(other, members)), device_id_type=mesh_ids)

    def send_fin(step, carry):
        fin_copy(step).start()
        return carry

    lax.fori_loop(1, members * side, send_fin, 0)
    others = fin.at[pl.ds(0, members * side - 1)]
    pltpu.make_async_copy(others, others, fin_recv).wait()

    for seq in range(seq_count):
        wanted = slots[seq]
        owner = lax.div(wanted, seq_count)
        inside = lax.rem(wanted, seq_count)
        found = fin[owner]
        turned = pltpu.roll(found, cap // 2, 1)
        found = jnp.where(inside >= half, turned, found)
        level = lax.rem(inside, half)
        row = lax.broadcasted_iota(jnp.int32, (half, cap), 0)
        gathered[pl.ds(seq, 1), :] = jnp.sum(jnp.where(row == level, found, 0.0), axis=0, keepdims=True)
    out[0] = gathered[:, 0:seq_len]
    out[1] = gathered[:, seq_len:2 * seq_len]

    def drain(index, carry):
        here = rows.at[0, pl.ds(0, piece_rows), :]
        pltpu.make_async_copy(here, here, row_send.at[index]).wait()
        return carry

    lax.fori_loop(0, len(row_plan), drain, 0)
    for (d, sub), link in weight_plan:
        weight_relay(d, sub, link).wait_send()
    for name in entries:
        entry_copy(name).wait_send()

    def drain_tags(index, carry):
        pltpu.make_async_copy(tags.at[0], tags.at[0], tag_send.at[index]).wait()
        return carry

    lax.fori_loop(0, len(tag_plan), drain_tags, 0)

    def drain_stats(index, carry):
        pltpu.make_async_copy(stats_in.at[0], stats_in.at[0], stat_send.at[index]).wait()
        return carry

    lax.fori_loop(1, sources, drain_stats, 0)
    pltpu.make_async_copy(others, others, fin_send).wait()


def local(hidden_states, norm_gain, head_weight, targets, lengths, slot_of):
    held, depth = hidden_states.shape
    seq_count = lengths.shape[0]
    seq_len = held // seq_count
    columns = head_weight.shape[1]
    members = 2 * side * side
    vmem = pl.BlockSpec(memory_space=pltpu.VMEM)
    smem = pl.BlockSpec(memory_space=pltpu.SMEM)
    dma = pltpu.SemaphoreType.DMA
    regular = pltpu.SemaphoreType.REGULAR
    out = jax.ShapeDtypeStruct((2, seq_count, seq_len), f32)
    both = pl.pallas_call(
        kernel,
        out_shape=out,
        in_specs=[smem, smem] + [pl.BlockSpec(memory_space=pl.ANY)] * 4,
        out_specs=vmem,
        scratch_shapes=[
            pltpu.VMEM((held, depth), jnp.bfloat16),
            pltpu.VMEM((1, depth), f32),
            pltpu.VMEM((1, held), jnp.int32),
            dma((3,)),
            pltpu.VMEM((part_count, part_height, depth), jnp.bfloat16),
            pltpu.VMEM((part_count, part_height, cap), jnp.int32),
            pltpu.VMEM((group_count, 2 * cap, depth), jnp.bfloat16),
            pltpu.VMEM((2 * group_count, 1, cap), jnp.int32),
            pltpu.VMEM((group_count, 2, 8, cap), f32),
            pltpu.VMEM((2 * group_count, 8, cap), f32),
            pltpu.VMEM((members * side, seq_count // 2, cap), f32),
            pltpu.VMEM((seq_count, cap), f32),
            dma((own_parts,)),
            dma((len(row_plan),)),
            dma((group_count * pieces,)),
            dma((group_count * pieces,)),
            dma((weight_sends,)),
            dma((rest_slots[-1] + 1,)),
            dma((len(tag_plan),)),
            dma((2 * group_count,)),
            dma((2 * group_count,)),
            dma,
            regular,
            regular,
            dma,
            dma,
        ],
        compiler_params=pltpu.CompilerParams(collective_id=0, has_side_effects=True, vmem_limit_bytes=60 << 20),
        name="head_stats",
    )(lengths, slot_of, hidden_states, norm_gain.reshape(1, depth), targets.reshape(1, held), head_weight.T)
    return (both[0], both[1])


def solution(mesh):
    rows = jax.sharding.PartitionSpec(("req", "vocab"), None)
    flat = jax.sharding.PartitionSpec(("req", "vocab"))
    in_specs = (rows, jax.sharding.PartitionSpec(), jax.sharding.PartitionSpec(None, "vocab"), flat, flat, flat)
    return jax.shard_map(local, mesh=mesh, in_specs=in_specs, out_specs=(rows, rows), check_vma=False)
```
